32 devices in a mesh: dp: 4 (over y, x), fsdp: 8 (over z, core).
Axes of the slice: x: 2, y: 2, z: 4, core: 2. Of those that a mesh axis runs over, the one named last changes fastest.
Arguments:
- tokens: bfloat16 [12288, 8192], P(('dp', 'fsdp')), may hold values from -6 to 6
- frozen_value_weight: bfloat16 [8192, 1024], P('fsdp'), may hold values from -0.0625 to 0.0625
- adapter_down_weight: bfloat16 [32, 8192, 64], P('dp', 'fsdp'), may hold values from -0.0625 to 0.0625
- adapter_up_weight: bfloat16 [32, 64, 1024], P('dp', None, 'fsdp'), may hold values from -0.75 to 0.75
- output_gradient: bfloat16 [12288, 1024], P(('dp', 'fsdp')), may hold values from -6 to 6
- adapter_per_block: int32 [96], P(('dp', 'fsdp')), may hold values from 0 to 31, as said below
- block_live_count: int32 [96], P(('dp', 'fsdp')), may hold values from 1 to 128
Outputs:
- values: bfloat16 [12288, 1024], P(('dp', 'fsdp'))
- input_gradient: bfloat16 [12288, 8192], P(('dp', 'fsdp'))
- grad_down: float32 [32, 8192, 64], P('dp', 'fsdp')
- grad_up: float32 [32, 64, 1024], P('dp', None, 'fsdp')
The draws below stay inside these ranges and needn't reach their ends.
Inputs may be any that keep to these rules, and one draw needn't show every extreme that they name: `adapter_per_block`: within the blocks of one device the adapter numbers never fall.
All inputs are finite; a program needn't handle non-finite values.
Results may differ from the reference program's by a relative error of at most 0.0038.
Values may be sent and summed in bfloat16 or wider, within the bound.
A program may use at most 192 MiB of HBM per device.

```python
import jax
import jax.numpy as jnp
from jax import lax

MODEL_WIDTH = 8192
VALUE_WIDTH = 1024
ADAPTER_RANK = 64
ADAPTER_COUNT = 32
BLOCK = 128
TOK_DEV = 384
TOKEN_SLOTS = 12288
N_BLOCKS = 96


def draw_adapter_per_block(key, part):
    per_dev = TOK_DEV // BLOCK
    groups = N_BLOCKS // per_dev
    upper_key, number_key, place_key = jax.random.split(jax.random.fold_in(key, 7), 3)
    upper = jax.random.randint(upper_key, (N_BLOCKS,), 1, ADAPTER_COUNT + 1)
    numbers = jax.random.randint(number_key, (N_BLOCKS,), 0, upper)
    ordered = jnp.sort(numbers.reshape(groups, per_dev), axis=1)
    ordered = ordered.at[0, 0].set(0)
    chosen = jax.random.randint(place_key, (), 1, groups)
    ordered = ordered.at[chosen, per_dev - 1].set(ADAPTER_COUNT - 1)
    return ordered.reshape(N_BLOCKS).astype(jnp.int32)


def set_ends(drawn, key, low, top_value):
    place = [jax.random.randint(jax.random.fold_in(key, axis), (), 0, length) for axis, length in enumerate(drawn.shape)]
    main_axis = drawn.shape.index(max(drawn.shape))
    beside = place[:main_axis] + [(place[main_axis] + 1) % drawn.shape[main_axis]] + place[main_axis + 1:]
    return drawn.at[tuple(place)].set(low).at[tuple(beside)].set(top_value)


def steps_of(own_key, shape, shards, low, top_value):
    loudness, own = 1.0, jax.random.fold_in(own_key, 6)
    for position, parts in shards:
        heights = jnp.exp(jax.random.uniform(jax.random.fold_in(own, position), (parts,), jnp.float32, low / len(shards), top_value / len(shards)))
        loudness = loudness * jnp.repeat(heights, shape[position] // parts).reshape([-1 if axis == position else 1 for axis in range(len(shape))])
    return loudness


def centred(rng, shape, spread, limit, shards=(), kind=jnp.bfloat16):
    drawn = jax.random.normal(rng, shape, jnp.float32) * spread
    if len(shards) > 0:
        drawn = steps_of(rng, shape, shards, -0.22, 0.18) * drawn
    return jnp.clip(drawn, min=-limit, max=limit).astype(kind)


def setup_inputs(seed: int = 0) -> dict:
    arg_keys = jax.random.split(jax.random.key(seed), 8)
    tokens = centred(arg_keys[0], (TOKEN_SLOTS, MODEL_WIDTH), 1.0, 6.0, ((0, 32),))
    frozen_value_weight = centred(arg_keys[1], (MODEL_WIDTH, VALUE_WIDTH), MODEL_WIDTH ** -0.5, 0.0625, ((0, 8),))
    adapter_down_weight = centred(arg_keys[2], (ADAPTER_COUNT, MODEL_WIDTH, ADAPTER_RANK), MODEL_WIDTH ** -0.5, 0.0625, ((0, 4), (1, 8)))
    adapter_up_weight = centred(arg_keys[3], (ADAPTER_COUNT, ADAPTER_RANK, VALUE_WIDTH), ADAPTER_RANK ** -0.5, 0.75, ((0, 4), (2, 8)))
    output_gradient = centred(arg_keys[4], (TOKEN_SLOTS, VALUE_WIDTH), 1.0, 6.0, ((0, 32),))
    adapter_per_block = draw_adapter_per_block(jax.random.fold_in(arg_keys[7], 71), 0)
    block_live_count = set_ends(jax.random.randint(arg_keys[6], (N_BLOCKS,), 1, BLOCK + 1), jax.random.fold_in(arg_keys[6], 1), 1, BLOCK).astype(jnp.int32)
    return {"tokens": tokens, "frozen_value_weight": frozen_value_weight, "adapter_down_weight": adapter_down_weight, "adapter_up_weight": adapter_up_weight, "output_gradient": output_gradient, "adapter_per_block": adapter_per_block, "block_live_count": block_live_count}


adapter_scale = 0.5


def reference(tokens, frozen_value_weight, adapter_down_weight, adapter_up_weight, output_gradient, adapter_per_block, block_live_count):
    frozen_output = jnp.dot(tokens, frozen_value_weight, preferred_element_type=jnp.float32)
    frozen_gradient = lax.dot_general(output_gradient, frozen_value_weight, (((1,), (1,)), ((), ())), preferred_element_type=jnp.float32)
    per_dev = TOK_DEV // BLOCK
    groups = N_BLOCKS // per_dev
    input_per_block = tokens.reshape(groups, per_dev, BLOCK, MODEL_WIDTH)
    dy_blocks = output_gradient.reshape(groups, per_dev, BLOCK, VALUE_WIDTH)
    ids = adapter_per_block.reshape(groups, per_dev)
    fills = block_live_count.reshape(groups, per_dev)
    positions = jnp.arange(BLOCK, dtype=jnp.int32)
    catalog = jnp.arange(ADAPTER_COUNT, dtype=jnp.int32)

    def one_device(carry, inputs):
        down_gradient_sum, up_gradient_sum = carry
        x_dev, dy_dev, adapter_index_local, fill_dev = inputs
        live_slot_mask = (positions[None, :] < fill_dev[:, None]).astype(jnp.float32)[:, :, None]
        down_per_block = adapter_down_weight[adapter_index_local].astype(jnp.float32)
        up_per_block = adapter_up_weight[adapter_index_local].astype(jnp.float32)
        input_gathered = x_dev.astype(jnp.float32)
        dy_wide = dy_dev.astype(jnp.float32)
        reduced_down_output = (jnp.einsum('gzq,gqx->gzx', input_gathered, down_per_block) * live_slot_mask).astype(jnp.bfloat16)
        reduced_output_gradient = (jnp.einsum('bkc,brc->bkr', dy_wide, up_per_block) * live_slot_mask).astype(jnp.bfloat16)
        raised_rows = jnp.einsum('bkr,brc->bkc', reduced_down_output.astype(jnp.float32), up_per_block).astype(jnp.bfloat16)
        collected_rows = jnp.einsum('qjz,qaz->qja', reduced_output_gradient.astype(jnp.float32), down_per_block).astype(jnp.bfloat16)
        choose = (adapter_index_local[:, None] == catalog[None, :]).astype(jnp.float32)
        up_terms = jnp.einsum('bkr,bkc->brc', reduced_down_output.astype(jnp.float32), dy_wide)
        down_gradient_terms = jnp.einsum('uia,uiw->uaw', input_gathered, reduced_output_gradient.astype(jnp.float32))
        down_gradient_sum = down_gradient_sum + jnp.einsum('ba,bdr->adr', choose, down_gradient_terms, precision=lax.Precision.HIGHEST)
        up_gradient_sum = up_gradient_sum + jnp.einsum('ba,brc->arc', choose, up_terms, precision=lax.Precision.HIGHEST)
        return (down_gradient_sum, up_gradient_sum), (raised_rows, collected_rows)

    start = (jnp.zeros((ADAPTER_COUNT, MODEL_WIDTH, ADAPTER_RANK), jnp.float32), jnp.zeros((ADAPTER_COUNT, ADAPTER_RANK, VALUE_WIDTH), jnp.float32))
    (down_gradient_sum, up_gradient_sum), (raised_rows, collected_rows) = lax.scan(one_device, start, (input_per_block, dy_blocks, ids, fills))
    values = (frozen_output + adapter_scale * raised_rows.reshape(TOKEN_SLOTS, VALUE_WIDTH).astype(jnp.float32)).astype(jnp.bfloat16)
    input_gradient = (frozen_gradient + adapter_scale * collected_rows.reshape(TOKEN_SLOTS, MODEL_WIDTH).astype(jnp.float32)).astype(jnp.bfloat16)
    return values, input_gradient, adapter_scale * down_gradient_sum, adapter_scale * up_gradient_sum
```

```python
import functools

import jax
import jax.numpy as jnp
from jax import lax
from jax.experimental import pallas as pl
from jax.experimental.pallas import tpu as pltpu
from jax.sharding import PartitionSpec as P

adapter_scale = 0.5
cores = 2
rows_chunk = 16
mesh_ids = pl.DeviceIdType.MESH


def dot(left, right, left_dim, right_dim):
    return lax.dot_general(
        left, right, (((left_dim,), (right_dim,)), ((), ())), preferred_element_type=jnp.float32
    )


def partner(position, offset, size):
    if size & (size - 1):
        return lax.rem(position + offset, size)
    bit = 1
    while bit < size:
        if offset & bit:
            position = position + bit - 2 * bit * lax.rem(position // bit, 2)
        bit *= 2
    return position


def kernel(
    dp, fsdp,
    ids_ref, fill_ref, pieces_ref, w_ref, x_hbm, dy_hbm,
    y_out, dx_out, down_out, up_out,
    x, dy, dy_slices, catalog, outgoing, arrived, returned, sums_in, frozen, id_rows,
    pick, put, u_rows, v_rows, u_cols, v_cols, up_blocks, total, dx_tiles, y_tile, down_tile, up_tile,
    load_sem, own_sem, s1_send, s1_recv, id_send, id_recv, p_send, p_recv, t_send, t_recv,
    g_send, g_recv, right_send, right_recv, left_send, left_recv, w2_send, w2_recv, w3_send, w3_recv,
    dx_sem, out_sem,
):
    my_dp, me = lax.axis_index("dp"), lax.axis_index("fsdp")
    chunks, _, own_rows, piece_width = catalog.shape
    per_dev, rank_rows, block_rows = u_rows.shape[1:]
    count_dev, model_width = x.shape
    width = dy.shape[1]
    features, outputs = model_width // fsdp, width // fsdp
    block_group = per_dev * rank_rows
    lanes = fsdp * block_group
    total_rows = dp * own_rows
    own = own_rows // rank_rows
    chips = fsdp // cores
    chip, core = me // cores, lax.rem(me, cores)
    tile_lanes = 384 if piece_width % 384 == 0 else piece_width

    def peer(offset):
        return lax.rem(me + offset, fsdp)

    def column(slice_index):
        return pl.ds(pl.multiple_of(slice_index * features, features), features)

    loads = [
        pltpu.make_async_copy(x_hbm, x, load_sem.at[0]),
        pltpu.make_async_copy(dy_hbm, dy, load_sem.at[1]),
        pltpu.make_async_copy(w_ref, frozen.at[me], load_sem.at[2]),
    ]
    owns = [
        pltpu.make_async_copy(pieces_ref.at[k], catalog.at[k, my_dp], own_sem.at[k])
        for k in range(chunks)
    ]

    lane_block = lax.shift_right_logical(
        lax.broadcasted_iota(jnp.int32, (8, lanes), 1), rank_rows.bit_length() - 1
    )
    mine = jnp.zeros((8, lanes), jnp.int32)
    for block in range(per_dev):
        mine = jnp.where(lane_block == me * per_dev + block, ids_ref[block] + 1, mine)
    id_rows[me] = mine

    barrier = pltpu.get_barrier_semaphore()

    @pl.loop(1, fsdp)
    def _(offset):
        pl.semaphore_signal(barrier, inc=1, device_id=(my_dp, peer(offset)), device_id_type=mesh_ids)

    for offset in range(1, dp):
        pl.semaphore_signal(
            barrier, inc=1, device_id=(partner(my_dp, offset, dp), me), device_id_type=mesh_ids
        )
    pl.semaphore_wait(barrier, fsdp + dp - 2)

    def remote(source, target, send, recv, device):
        return pltpu.make_async_remote_copy(
            src_ref=source, dst_ref=target, send_sem=send, recv_sem=recv,
            device_id=device, device_id_type=mesh_ids,
        )

    def id_copy(offset):
        return remote(
            id_rows.at[me], id_rows.at[me], id_send.at[offset], id_recv.at[offset],
            (my_dp, peer(offset)),
        )

    def s1_copy(k, offset):
        return remote(
            pieces_ref.at[k], catalog.at[k, my_dp], s1_send.at[k, offset], s1_recv.at[k, offset],
            (partner(my_dp, offset, dp), me),
        )

    def p_copy(k, offset):
        return remote(
            outgoing.at[k, peer(offset)], arrived.at[k, me], p_send.at[k, offset],
            p_recv.at[k, offset], (my_dp, peer(offset)),
        )

    def t_copy(k, offset):
        return remote(
            outgoing.at[k, peer(offset)], returned.at[k, me], t_send.at[k, offset],
            t_recv.at[k, offset], (my_dp, peer(offset)),
        )

    def g_copy(k, offset):
        other = partner(my_dp, offset, dp)
        return remote(
            catalog.at[k, other], sums_in.at[k, my_dp], g_send.at[k, offset], g_recv.at[k, offset],
            (other, me),
        )

    def right_copy(step):
        source = w_ref.at[my_dp] if step == 0 else frozen.at[me - cores * step, my_dp]
        return remote(
            source, frozen.at[me - cores * step, my_dp], right_send.at[step], right_recv.at[step],
            (my_dp, me + cores),
        )

    def left_copy(step):
        source = w_ref.at[my_dp] if step == 0 else frozen.at[me + cores * step, my_dp]
        return remote(
            source, frozen.at[me + cores * step, my_dp], left_send.at[step], left_recv.at[step],
            (my_dp, me - cores),
        )

    def sends_right(step):
        return (chip >= step) & (chip + 1 < chips)

    def sends_left(step):
        return (chip + step < chips) & (chip >= 1)

    def gets_right(step):
        return chip >= step + 1

    def gets_left(step):
        return chip + step + 1 < chips

    def w2_copy(from_chip, offset):
        row = from_chip * cores + core
        return remote(
            frozen.at[row, my_dp], frozen.at[row, my_dp], w2_send.at[from_chip, offset],
            w2_recv.at[from_chip, offset], (partner(my_dp, offset, dp), me),
        )

    def w3_copy(from_chip):
        row = from_chip * cores + core
        return remote(
            frozen.at[row], frozen.at[row], w3_send.at[from_chip], w3_recv.at[from_chip],
            (my_dp, me + 1 - 2 * core),
        )

    def relay(step):
        @pl.when(gets_right(step))
        def _():
            right_copy(step).wait_recv()

        @pl.when(gets_left(step))
        def _():
            left_copy(step).wait_recv()

        if step + 1 < chips - 1:

            @pl.when(sends_right(step + 1))
            def _():
                right_copy(step + 1).start()

            @pl.when(sends_left(step + 1))
            def _():
                left_copy(step + 1).start()

    def spread_shares(step):
        @pl.when(gets_right(step))
        def _():
            for offset in range(1, dp):
                w2_copy(chip - step - 1, offset).start()

        @pl.when(gets_left(step))
        def _():
            for offset in range(1, dp):
                w2_copy(chip + step + 1, offset).start()

    @pl.loop(1, fsdp)
    def _(offset):
        id_copy(offset).start()

    for offset in range(1, dp):
        s1_copy(0, offset).start()

    @pl.when(sends_right(0))
    def _():
        right_copy(0).start()

    @pl.when(sends_left(0))
    def _():
        left_copy(0).start()

    for k in range(1, chunks):
        for offset in range(1, dp):
            s1_copy(k, offset).start()
    for copy in owns + loads:
        copy.start()

    @pl.loop(1, fsdp)
    def _(offset):
        id_copy(offset).wait_recv()

    numbers = id_rows[0]
    for position in range(1, fsdp):
        numbers = numbers + id_rows[position]
    numbers = numbers[0:1, :] - 1
    shift = rank_rows.bit_length() - 1
    row = lax.broadcasted_iota(jnp.int32, (total_rows, lanes), 0)
    lane = lax.broadcasted_iota(jnp.int32, (total_rows, lanes), 1)
    same_rank = (row & (rank_rows - 1)) == (lane & (rank_rows - 1))
    same_adapter = lax.shift_right_logical(row, shift) == numbers
    hot = jnp.where(same_rank & same_adapter, 1.0, 0.0)
    put[...] = hot.astype(jnp.bfloat16)
    pick[...] = hot.T.astype(jnp.bfloat16)

    def choose(k):
        owns[k].wait()
        for offset in range(1, dp):
            s1_copy(k, offset).wait_recv()
        for start in range(0, piece_width, tile_lanes):
            table = catalog[k, :, :, start : start + tile_lanes].reshape(total_rows, tile_lanes)
            chosen = dot(pick[...], table, 1, 0).astype(jnp.bfloat16)
            outgoing[k, :, :, start : start + tile_lanes] = chosen.reshape(
                fsdp, block_group, tile_lanes
            )
        arrived[k, me] = outgoing[k, me]

        @pl.loop(1, fsdp)
        def _(offset):
            p_copy(k, offset).start()

    def low_rank(k):
        @pl.loop(1, fsdp)
        def _(offset):
            p_copy(k, offset).wait_recv()

        zero = jnp.zeros((rank_rows, block_rows), jnp.float32)

        def gather_low(index, sums):
            result = []
            for block in range(per_dev):
                tokens = slice(block * block_rows, (block + 1) * block_rows)
                ranks = slice(block * rank_rows, (block + 1) * rank_rows)
                u = dot(arrived[k, index, ranks, :features], x[tokens, column(index)], 1, 1)
                v = dot(arrived[k, index, ranks, features:], dy_slices[index, tokens, :], 1, 1)
                result += [sums[2 * block] + u, sums[2 * block + 1] + v]
            return tuple(result)

        sums = lax.fori_loop(0, fsdp, gather_low, (zero,) * (2 * per_dev))
        token = lax.broadcasted_iota(jnp.int32, (rank_rows, block_rows), 1)
        for block in range(per_dev):
            live = (token < fill_ref[block]).astype(jnp.float32)
            u_rows[k, block] = (sums[2 * block] * live).astype(jnp.bfloat16)
            v_rows[k, block] = (sums[2 * block + 1] * live).astype(jnp.bfloat16)

        def terms_of(index):
            for block in range(per_dev):
                tokens = slice(block * block_rows, (block + 1) * block_rows)
                ranks = slice(block * rank_rows, (block + 1) * rank_rows)
                down = dot(v_rows[k, block], x[tokens, column(index)], 1, 0)
                up = dot(u_rows[k, block], dy_slices[index, tokens, :], 1, 0)
                outgoing[k, index, ranks, :features] = down.astype(jnp.bfloat16)
                outgoing[k, index, ranks, features:] = up.astype(jnp.bfloat16)

        @pl.loop(1, fsdp)
        def _(offset):
            p_copy(k, offset).wait_send()

        @pl.loop(1, fsdp)
        def _(offset):
            terms_of(peer(offset))

            @pl.when(offset > 1)
            def _():
                t_copy(k, offset - 1).start()

        terms_of(me)
        t_copy(k, fsdp - 1).start()
        returned[k, me] = outgoing[k, me]

    def combine(k):
        @pl.loop(1, fsdp)
        def _(offset):
            t_copy(k, offset).wait_recv()

        for start in range(0, piece_width, tile_lanes):
            terms = returned[k, :, :, start : start + tile_lanes].reshape(lanes, tile_lanes)
            added = dot(put[...], terms, 1, 0).astype(jnp.bfloat16)
            catalog[k, :, :, start : start + tile_lanes] = added.reshape(dp, own_rows, tile_lanes)
        for offset in range(1, dp):
            g_copy(k, offset).start()
        sums_in[k, my_dp] = catalog[k, my_dp]

    def out_copies(k):
        part = pl.ds(k * rank_rows, rank_rows)
        return (
            pltpu.make_async_copy(down_tile.at[k], down_out.at[:, part, :], out_sem.at[0, k]),
            pltpu.make_async_copy(up_tile.at[k], up_out.at[:, part, :], out_sem.at[1, k]),
        )

    def finish(k):
        for offset in range(1, dp):
            g_copy(k, offset).wait_recv()
        added = sums_in[k, 0].astype(jnp.float32)
        for position in range(1, dp):
            added = added + sums_in[k, position].astype(jnp.float32)
        added = adapter_scale * added
        down_tile[k] = added[:, :features].reshape(own, rank_rows, features)
        up_tile[k] = added[:, features:].reshape(own, rank_rows, outputs)
        for copy in out_copies(k):
            copy.start()

    def columns_of_low():
        for block in range(per_dev):
            for rows, columns in ((u_rows, u_cols), (v_rows, v_cols)):
                whole = jnp.concatenate([rows[k, block] for k in range(chunks)], axis=0)
                columns[block] = whole.astype(jnp.float32).T.astype(jnp.bfloat16)
            for index in range(fsdp):
                part = slice(index * outputs, (index + 1) * outputs)
                ranks = slice(block * rank_rows, (block + 1) * rank_rows)
                for k in range(chunks):
                    up_blocks[block, k * rank_rows : (k + 1) * rank_rows, part] = arrived[
                        k, index, ranks, features:
                    ]

    def dx_copy(index):
        slot = lax.rem(index, 2)
        return pltpu.make_async_copy(dx_tiles.at[slot], dx_out.at[:, column(index)], dx_sem.at[slot])

    def base(first, last):
        @pl.loop(first, last)
        def _(index):
            weight = frozen[index].reshape(features, width)
            product = dot(x[:, column(index)], weight, 1, 0)

            @pl.when(index == 0)
            def _():
                total[...] = product

            @pl.when(index > 0)
            def _():
                total[...] += product

            base_grad = dot(dy[...], weight, 1, 1)

            @pl.when(index >= 2)
            def _():
                dx_copy(index - 2).wait()

            slot = lax.rem(index, 2)
            for block in range(per_dev):
                tokens = slice(block * block_rows, (block + 1) * block_rows)
                ranks = slice(block * rank_rows, (block + 1) * rank_rows)
                down = jnp.concatenate(
                    [arrived[k, index, ranks, :features] for k in range(chunks)], axis=0
                )
                pulled = dot(v_cols[block], down, 1, 0).astype(jnp.bfloat16).astype(jnp.float32)
                dx_tiles[slot, tokens, :] = (base_grad[tokens, :] + adapter_scale * pulled).astype(
                    jnp.bfloat16
                )
            dx_copy(index).start()

    y_copy = pltpu.make_async_copy(y_tile, y_out, load_sem.at[0])

    def last_values():
        for block in range(per_dev):
            tokens = slice(block * block_rows, (block + 1) * block_rows)
            lifted = dot(u_cols[block], up_blocks[block], 1, 0)
            lifted = lifted.astype(jnp.bfloat16).astype(jnp.float32)
            y_tile[tokens, :] = (total[tokens, :] + adapter_scale * lifted).astype(jnp.bfloat16)
        y_copy.start()

    hops = chips - 1
    relayed = 0
    choose(0)
    relay(0)
    choose(1)
    for copy in loads:
        copy.wait()
    for index in range(fsdp):
        dy_slices[index] = dy[:, index * outputs : (index + 1) * outputs]
    for k in range(2, chunks):
        choose(k)
    spread_shares(0)
    low_rank(0)
    for step in range(1, hops):
        relay(step)
        spread_shares(step)
    for k in range(1, chunks):
        low_rank(k)
        if k >= 2:
            combine(k - 2)
    columns_of_low()

    def w2_done(from_chip):
        @pl.when(from_chip != chip)
        def _():
            for offset in range(1, dp):
                w2_copy(from_chip, offset).wait_recv()

    for from_chip in range(chips):
        w2_done(from_chip)
        w3_copy(from_chip).start()
    for from_chip in range(chips):
        w3_copy(from_chip).wait_recv()
    base(0, fsdp // 2)
    combine(chunks - 2)
    base(fsdp // 2, fsdp)
    last_values()
    for k in range(chunks - 2):
        finish(k)
    combine(chunks - 1)
    finish(chunks - 2)
    finish(chunks - 1)

    @pl.loop(1, fsdp)
    def _(offset):
        id_copy(offset).wait_send()
        for k in range(chunks):
            t_copy(k, offset).wait_send()

    for k in range(chunks):
        for offset in range(1, dp):
            s1_copy(k, offset).wait_send()
            g_copy(k, offset).wait_send()
        for copy in out_copies(k):
            copy.wait()
    for step in range(hops):

        @pl.when(sends_right(step))
        def _():
            right_copy(step).wait_send()

        @pl.when(sends_left(step))
        def _():
            left_copy(step).wait_send()

    for from_chip in range(chips):

        @pl.when(from_chip != chip)
        def _():
            for offset in range(1, dp):
                w2_copy(from_chip, offset).wait_send()

        w3_copy(from_chip).wait_send()
    for index in (fsdp - 2, fsdp - 1):
        dx_copy(index).wait()
    y_copy.wait()


def body(
    tokens,
    frozen_value_weight,
    adapter_down_weight,
    adapter_up_weight,
    output_gradient,
    adapter_per_block,
    block_live_count,
):
    dp, fsdp = lax.axis_size("dp"), lax.axis_size("fsdp")
    count_dev, model_width = tokens.shape
    width = output_gradient.shape[1]
    per_dev = adapter_per_block.shape[0]
    block_rows = count_dev // per_dev
    own, features, rank = adapter_down_weight.shape
    outputs = adapter_up_weight.shape[2]
    piece_width = features + outputs
    chunks = rank // rows_chunk
    chips = fsdp // cores
    share_rows = frozen_value_weight.shape[0] // dp
    pieces = jnp.concatenate([adapter_down_weight.transpose(0, 2, 1), adapter_up_weight], axis=2)
    pieces = pieces.reshape(own, chunks, rows_chunk, piece_width).transpose(1, 0, 2, 3)
    pieces = pieces.reshape(chunks, own * rows_chunk, piece_width)
    weight = frozen_value_weight.reshape(dp, share_rows, width)
    block_group = per_dev * rows_chunk
    lanes = fsdp * block_group
    total_rows = dp * own * rows_chunk
    bf16, f32 = jnp.bfloat16, jnp.float32
    anywhere = pl.BlockSpec(memory_space=pl.ANY)
    scalars = pl.BlockSpec(memory_space=pltpu.SMEM)
    dma = pltpu.SemaphoreType.DMA
    scratch = [
        pltpu.VMEM((count_dev, model_width), bf16),
        pltpu.VMEM((count_dev, width), bf16),
        pltpu.VMEM((fsdp, count_dev, outputs), bf16),
        pltpu.VMEM((chunks, dp, own * rows_chunk, piece_width), bf16),
        pltpu.VMEM((chunks, fsdp, block_group, piece_width), bf16),
        pltpu.VMEM((chunks, fsdp, block_group, piece_width), bf16),
        pltpu.VMEM((chunks, fsdp, block_group, piece_width), bf16),
        pltpu.VMEM((chunks, dp, own * rows_chunk, piece_width), bf16),
        pltpu.VMEM((fsdp, dp, share_rows, width), bf16),
        pltpu.VMEM((fsdp, 8, lanes), jnp.int32),
        pltpu.VMEM((lanes, total_rows), bf16),
        pltpu.VMEM((total_rows, lanes), bf16),
        pltpu.VMEM((chunks, per_dev, rows_chunk, block_rows), bf16),
        pltpu.VMEM((chunks, per_dev, rows_chunk, block_rows), bf16),
        pltpu.VMEM((per_dev, block_rows, rank), bf16),
        pltpu.VMEM((per_dev, block_rows, rank), bf16),
        pltpu.VMEM((per_dev, rank, width), bf16),
        pltpu.VMEM((count_dev, width), f32),
        pltpu.VMEM((2, count_dev, features), bf16),
        pltpu.VMEM((count_dev, width), bf16),
        pltpu.VMEM((chunks, own, rows_chunk, features), f32),
        pltpu.VMEM((chunks, own, rows_chunk, outputs), f32),
        dma((3,)),
        dma((chunks,)),
        dma((chunks, dp)), dma((chunks, dp)),
        dma((fsdp,)), dma((fsdp,)),
        dma((chunks, fsdp)), dma((chunks, fsdp)),
        dma((chunks, fsdp)), dma((chunks, fsdp)),
        dma((chunks, dp)), dma((chunks, dp)),
        dma((chips,)), dma((chips,)),
        dma((chips,)), dma((chips,)),
        dma((chips, dp)), dma((chips, dp)),
        dma((chips,)), dma((chips,)),
        dma((2,)),
        dma((2, chunks)),
    ]
    values, input_gradient, grad_down, grad_up = pl.pallas_call(
        functools.partial(kernel, dp, fsdp),
        out_shape=(
            jax.ShapeDtypeStruct((count_dev, width), bf16),
            jax.ShapeDtypeStruct((count_dev, model_width), bf16),
            jax.ShapeDtypeStruct((own, rank, features), f32),
            jax.ShapeDtypeStruct((own, rank, outputs), f32),
        ),
        in_specs=[scalars, scalars] + [anywhere] * 4,
        out_specs=(anywhere,) * 4,
        scratch_shapes=scratch,
        compiler_params=pltpu.CompilerParams(
            collective_id=0, has_side_effects=True, vmem_limit_bytes=66_000_000
        ),
        name="lora",
    )(adapter_per_block, block_live_count, pieces, weight, tokens, output_gradient)
    return values, input_gradient, grad_down.transpose(0, 2, 1), grad_up


def solution(mesh):
    placed = (
        P(("dp", "fsdp"), None),
        P("fsdp", None),
        P("dp", "fsdp", None),
        P("dp", None, "fsdp"),
        P(("dp", "fsdp"), None),
        P(("dp", "fsdp")),
        P(("dp", "fsdp")),
    )
    return jax.shard_map(
        body,
        mesh=mesh,
        in_specs=placed,
        out_specs=(
            P(("dp", "fsdp"), None),
            P(("dp", "fsdp"), None),
            P("dp", "fsdp", None),
            P("dp", None, "fsdp"),
        ),
        check_vma=False,
    )
```

```python
import functools

import jax
import jax.numpy as jnp
from jax import lax
from jax.experimental import pallas as pl
from jax.experimental.pallas import tpu as pltpu
from jax.sharding import PartitionSpec as P

adapter_scale = 0.5
cores = 2
rows_chunk = 16
mesh_ids = pl.DeviceIdType.MESH


def dot(left, right, left_dim, right_dim):
    return lax.dot_general(
        left, right, (((left_dim,), (right_dim,)), ((), ())), preferred_element_type=jnp.float32
    )


def partner(position, offset, size):
    if size & (size - 1):
        return lax.rem(position + offset, size)
    bit = 1
    while bit < size:
        if offset & bit:
            position = position + bit - 2 * bit * lax.rem(position // bit, 2)
        bit *= 2
    return position


def lane_tile(piece_width):
    return 384 if piece_width % 384 == 0 else piece_width


def kernel(
    dp, fsdp,
    ids_ref, fill_ref, down_ref, up_ref, w_ref, x_hbm, dy_hbm,
    y_out, dx_out, down_out, up_out,
    x, dy, dy_slices, catalog, outgoing, arrived, returned, sums_in, frozen, id_rows,
    pick, put, u_rows, v_rows, u_cols, v_cols, up_blocks, total,
    load_sem, own_sem, s1_send, s1_recv, id_send, id_recv, p_send, p_recv, t_send, t_recv,
    g_send, g_recv, right_send, right_recv, left_send, left_recv, w2_send, w2_recv, w3_send, w3_recv,
):
    my_dp, me = lax.axis_index("dp"), lax.axis_index("fsdp")
    chunks, _, own, _, piece_width = catalog.shape
    per_dev, rank_rows, block_rows = u_rows.shape[1:]
    count_dev, model_width = x.shape
    width = dy.shape[1]
    features, outputs = model_width // fsdp, width // fsdp
    block_group = per_dev * rank_rows
    lanes = fsdp * block_group
    total_rows = dp * own * rank_rows
    chips = fsdp // cores
    chip, core = me // cores, lax.rem(me, cores)
    tile_lanes = lane_tile(piece_width)
    parts = piece_width // tile_lanes
    last = chunks - 1

    def peer(offset):
        return lax.rem(me + offset, fsdp)

    def column(slice_index):
        return pl.ds(pl.multiple_of(slice_index * features, features), features)

    loads = [
        pltpu.make_async_copy(x_hbm, x, load_sem.at[0]),
        pltpu.make_async_copy(dy_hbm, dy, load_sem.at[1]),
        pltpu.make_async_copy(w_ref, frozen.at[me], load_sem.at[2]),
    ]
    owns = []
    for k in range(chunks):
        ranks = pl.ds(k * rank_rows, rank_rows)
        place = catalog.at[k, my_dp]
        if outputs % 128 == 0:
            owns.append((
                pltpu.make_async_copy(
                    down_ref.at[:, ranks, :], place.at[:, :, pl.ds(0, features)], own_sem.at[0, k]
                ),
                pltpu.make_async_copy(
                    up_ref.at[:, ranks, :], place.at[:, :, pl.ds(features, outputs)], own_sem.at[1, k]
                ),
            ))
        else:
            owns.append((pltpu.make_async_copy(down_ref.at[:, ranks, :], place, own_sem.at[0, k]),))
    for copies in owns:
        for copy in copies:
            copy.start()

    lane_block = lax.shift_right_logical(
        lax.broadcasted_iota(jnp.int32, (8, lanes), 1), rank_rows.bit_length() - 1
    )
    mine = jnp.zeros((8, lanes), jnp.int32)
    for block in range(per_dev):
        mine = jnp.where(lane_block == me * per_dev + block, ids_ref[block] + 1, mine)
    id_rows[me] = mine

    barrier = pltpu.get_barrier_semaphore()

    @pl.loop(1, fsdp)
    def _(offset):
        pl.semaphore_signal(barrier, inc=1, device_id=(my_dp, peer(offset)), device_id_type=mesh_ids)

    for offset in range(1, dp):
        pl.semaphore_signal(
            barrier, inc=1, device_id=(partner(my_dp, offset, dp), me), device_id_type=mesh_ids
        )
    pl.semaphore_wait(barrier, fsdp + dp - 2)

    def remote(source, target, send, recv, device):
        return pltpu.make_async_remote_copy(
            src_ref=source, dst_ref=target, send_sem=send, recv_sem=recv,
            device_id=device, device_id_type=mesh_ids,
        )

    def id_copy(offset):
        return remote(
            id_rows.at[me], id_rows.at[me], id_send.at[offset], id_recv.at[offset],
            (my_dp, peer(offset)),
        )

    def s1_copy(k, offset):
        return remote(
            catalog.at[k, my_dp], catalog.at[k, my_dp], s1_send.at[k, offset], s1_recv.at[k, offset],
            (partner(my_dp, offset, dp), me),
        )

    def p_copy(k, offset):
        return remote(
            outgoing.at[k, peer(offset)], arrived.at[k, me], p_send.at[k, offset],
            p_recv.at[k, offset], (my_dp, peer(offset)),
        )

    def lanes_of(k, part):
        return pl.ds(0, piece_width) if k < last else pl.ds(part * tile_lanes, tile_lanes)

    def t_copy(k, offset, part=0):
        sent = lanes_of(k, part)
        return remote(
            outgoing.at[k, peer(offset), :, sent], returned.at[k, me, :, sent],
            t_send.at[k + part, offset], t_recv.at[k + part, offset], (my_dp, peer(offset)),
        )

    def g_copy(k, offset, part=0):
        other = partner(my_dp, offset, dp)
        sent = lanes_of(k, part)
        return remote(
            catalog.at[k, other, :, :, sent], sums_in.at[k, my_dp, :, :, sent],
            g_send.at[k + part, offset], g_recv.at[k + part, offset], (other, me),
        )

    def parts_of(k):
        return range(parts) if k == last else range(1)

    def right_copy(step):
        source = w_ref.at[my_dp] if step == 0 else frozen.at[me - cores * step, my_dp]
        return remote(
            source, frozen.at[me - cores * step, my_dp], right_send.at[step], right_recv.at[step],
            (my_dp, me + cores),
        )

    def left_copy(step):
        source = w_ref.at[my_dp] if step == 0 else frozen.at[me + cores * step, my_dp]
        return remote(
            source, frozen.at[me + cores * step, my_dp], left_send.at[step], left_recv.at[step],
            (my_dp, me - cores),
        )

    def sends_right(step):
        return (chip >= step) & (chip + 1 < chips)

    def sends_left(step):
        return (chip + step < chips) & (chip >= 1)

    def gets_right(step):
        return chip >= step + 1

    def gets_left(step):
        return chip + step + 1 < chips

    def w2_copy(from_chip, offset):
        row = from_chip * cores + core
        return remote(
            frozen.at[row, my_dp], frozen.at[row, my_dp], w2_send.at[from_chip, offset],
            w2_recv.at[from_chip, offset], (partner(my_dp, offset, dp), me),
        )

    def w3_copy(from_chip):
        row = from_chip * cores + core
        return remote(
            frozen.at[row], frozen.at[row], w3_send.at[from_chip], w3_recv.at[from_chip],
            (my_dp, me + 1 - 2 * core),
        )

    def relay(step):
        @pl.when(gets_right(step))
        def _():
            right_copy(step).wait_recv()

        @pl.when(gets_left(step))
        def _():
            left_copy(step).wait_recv()

        if step + 1 < chips - 1:

            @pl.when(sends_right(step + 1))
            def _():
                right_copy(step + 1).start()

            @pl.when(sends_left(step + 1))
            def _():
                left_copy(step + 1).start()

    def spread_shares(step):
        @pl.when(gets_right(step))
        def _():
            for offset in range(1, dp):
                w2_copy(chip - step - 1, offset).start()

        @pl.when(gets_left(step))
        def _():
            for offset in range(1, dp):
                w2_copy(chip + step + 1, offset).start()

    @pl.loop(1, fsdp)
    def _(offset):
        id_copy(offset).start()

    def share_catalog(k):
        for copy in owns[k]:
            copy.wait()
        for offset in range(1, dp):
            s1_copy(k, offset).start()

    share_catalog(0)

    @pl.when(sends_right(0))
    def _():
        right_copy(0).start()

    @pl.when(sends_left(0))
    def _():
        left_copy(0).start()

    for k in range(1, chunks):
        share_catalog(k)
    for copy in loads:
        copy.start()

    @pl.loop(1, fsdp)
    def _(offset):
        id_copy(offset).wait_recv()

    numbers = id_rows[0]
    for position in range(1, fsdp):
        numbers = numbers + id_rows[position]
    numbers = numbers[0:1, :] - 1
    shift = rank_rows.bit_length() - 1
    row = lax.broadcasted_iota(jnp.int32, (total_rows, lanes), 0)
    lane = lax.broadcasted_iota(jnp.int32, (total_rows, lanes), 1)
    same_rank = (row & (rank_rows - 1)) == (lane & (rank_rows - 1))
    same_adapter = lax.shift_right_logical(row, shift) == numbers
    hot = jnp.where(same_rank & same_adapter, 1.0, 0.0)
    put[...] = hot.astype(jnp.bfloat16)
    pick[...] = hot.T.astype(jnp.bfloat16)

    def choose(k):
        for offset in range(1, dp):
            s1_copy(k, offset).wait_recv()
        for start in range(0, piece_width, tile_lanes):
            table = catalog[k, :, :, :, start : start + tile_lanes].reshape(total_rows, tile_lanes)
            chosen = dot(pick[...], table, 1, 0).astype(jnp.bfloat16)
            outgoing[k, :, :, start : start + tile_lanes] = chosen.reshape(
                fsdp, block_group, tile_lanes
            )
        arrived[k, me] = outgoing[k, me]

        @pl.loop(1, fsdp)
        def _(offset):
            p_copy(k, offset).start()

    def low_rank(k):
        @pl.loop(1, fsdp)
        def _(offset):
            p_copy(k, offset).wait_recv()

        zero = jnp.zeros((rank_rows, block_rows), jnp.float32)

        def gather_low(index, sums):
            result = []
            for block in range(per_dev):
                tokens = slice(block * block_rows, (block + 1) * block_rows)
                ranks = slice(block * rank_rows, (block + 1) * rank_rows)
                u = dot(arrived[k, index, ranks, :features], x[tokens, column(index)], 1, 1)
                v = dot(arrived[k, index, ranks, features:], dy_slices[index, tokens, :], 1, 1)
                result += [sums[2 * block] + u, sums[2 * block + 1] + v]
            return tuple(result)

        sums = lax.fori_loop(0, fsdp, gather_low, (zero,) * (2 * per_dev))
        token = lax.broadcasted_iota(jnp.int32, (rank_rows, block_rows), 1)
        for block in range(per_dev):
            live = (token < fill_ref[block]).astype(jnp.float32)
            u_rows[k, block] = (sums[2 * block] * live).astype(jnp.bfloat16)
            v_rows[k, block] = (sums[2 * block + 1] * live).astype(jnp.bfloat16)

        def terms_of(index):
            for block in range(per_dev):
                tokens = slice(block * block_rows, (block + 1) * block_rows)
                ranks = slice(block * rank_rows, (block + 1) * rank_rows)
                down = dot(v_rows[k, block], x[tokens, column(index)], 1, 0)
                up = dot(u_rows[k, block], dy_slices[index, tokens, :], 1, 0)
                outgoing[k, index, ranks, :features] = down.astype(jnp.bfloat16)
                outgoing[k, index, ranks, features:] = up.astype(jnp.bfloat16)

        @pl.loop(1, fsdp)
        def _(offset):
            p_copy(k, offset).wait_send()

        @pl.loop(1, fsdp)
        def _(offset):
            terms_of(peer(offset))
            if k < last:

                @pl.when(offset > 1)
                def _():
                    t_copy(k, offset - 1).start()

        terms_of(me)
        if k < last:
            t_copy(k, fsdp - 1).start()
        else:
            for part in parts_of(k):

                @pl.loop(1, fsdp)
                def _(offset):
                    t_copy(k, offset, part).start()

        returned[k, me] = outgoing[k, me]

    def combine(k, part=0):
        if part == 0:
            for offset in range(1, dp):
                s1_copy(k, offset).wait_send()

        @pl.loop(1, fsdp)
        def _(offset):
            t_copy(k, offset, part).wait_recv()

        starts = [part * tile_lanes] if k == last else range(0, piece_width, tile_lanes)
        for start in starts:
            tile = slice(start, start + tile_lanes)
            terms = returned[k, :, :, tile].reshape(lanes, tile_lanes)
            added = dot(put[...], terms, 1, 0).astype(jnp.bfloat16)
            catalog[k, :, :, :, tile] = added.reshape(dp, own, rank_rows, tile_lanes)
        for offset in range(1, dp):
            g_copy(k, offset, part).start()
        for start in starts:
            tile = slice(start, start + tile_lanes)
            sums_in[k, my_dp, :, :, tile] = catalog[k, my_dp, :, :, tile]

    def finish(k):
        for part in parts_of(k):
            for offset in range(1, dp):
                g_copy(k, offset, part).wait_recv()
        added = sums_in[k, 0].astype(jnp.float32)
        for position in range(1, dp):
            added = added + sums_in[k, position].astype(jnp.float32)
        added = adapter_scale * added
        ranks = slice(k * rank_rows, (k + 1) * rank_rows)
        down_out[:, ranks, :] = added[:, :, :features]
        up_out[:, ranks, :] = added[:, :, features:]

    def columns_of_low():
        for block in range(per_dev):
            for rows, columns in ((u_rows, u_cols), (v_rows, v_cols)):
                whole = jnp.concatenate([rows[k, block] for k in range(chunks)], axis=0)
                columns[block] = whole.astype(jnp.float32).T.astype(jnp.bfloat16)
            for index in range(fsdp):
                part = slice(index * outputs, (index + 1) * outputs)
                ranks = slice(block * rank_rows, (block + 1) * rank_rows)
                for k in range(chunks):
                    up_blocks[block, k * rank_rows : (k + 1) * rank_rows, part] = arrived[
                        k, index, ranks, features:
                    ]

    def base_values():
        @pl.loop(0, fsdp)
        def _(index):
            product = dot(x[:, column(index)], frozen[index].reshape(features, width), 1, 0)

            @pl.when(index == 0)
            def _():
                total[...] = product

            @pl.when(index > 0)
            def _():
                total[...] += product

    def base_grads(first, end):
        @pl.loop(first, end)
        def _(index):
            base_grad = dot(dy[...], frozen[index].reshape(features, width), 1, 1)
            for block in range(per_dev):
                tokens = slice(block * block_rows, (block + 1) * block_rows)
                ranks = slice(block * rank_rows, (block + 1) * rank_rows)
                down = jnp.concatenate(
                    [arrived[k, index, ranks, :features] for k in range(chunks)], axis=0
                )
                pulled = dot(v_cols[block], down, 1, 0).astype(jnp.bfloat16).astype(jnp.float32)
                mixed = base_grad[tokens, :] + adapter_scale * pulled
                dx_out[tokens, column(index)] = mixed.astype(jnp.bfloat16)

    def last_values():
        for block in range(per_dev):
            tokens = slice(block * block_rows, (block + 1) * block_rows)
            lifted = dot(u_cols[block], up_blocks[block], 1, 0)
            lifted = lifted.astype(jnp.bfloat16).astype(jnp.float32)
            y_out[tokens, :] = (total[tokens, :] + adapter_scale * lifted).astype(jnp.bfloat16)

    def pass_core(step):
        def give(from_chip):
            for offset in range(1, dp):
                w2_copy(from_chip, offset).wait_recv()
            w3_copy(from_chip).start()

        @pl.when(gets_right(step))
        def _():
            give(chip - step - 1)

        @pl.when(gets_left(step))
        def _():
            give(chip + step + 1)

    hops = chips - 1
    relay(0)
    choose(0)
    spread_shares(0)
    for copy in loads:
        copy.wait()
    w3_copy(chip).start()
    for index in range(fsdp):
        dy_slices[index] = dy[:, index * outputs : (index + 1) * outputs]
    choose(1)
    low_rank(0)
    for step in range(1, hops):
        relay(step)
        spread_shares(step)
    choose(2)
    low_rank(1)
    pass_core(0)
    for k in range(3, chunks):
        choose(k)
        combine(k - 3)
        low_rank(k - 1)
    for step in range(1, hops):
        pass_core(step)
    for from_chip in range(chips):
        w3_copy(from_chip).wait_recv()
    base_values()
    combine(chunks - 3)
    low_rank(last)
    columns_of_low()
    base_grads(0, fsdp)
    last_values()
    combine(last - 1)
    for part in parts_of(last):
        combine(last, part)
    for k in range(chunks):
        finish(k)

    @pl.loop(1, fsdp)
    def _(offset):
        id_copy(offset).wait_send()
        for k in range(chunks):
            for part in parts_of(k):
                t_copy(k, offset, part).wait_send()

    for k in range(chunks):
        for offset in range(1, dp):
            for part in parts_of(k):
                g_copy(k, offset, part).wait_send()
    for step in range(hops):

        @pl.when(sends_right(step))
        def _():
            right_copy(step).wait_send()

        @pl.when(sends_left(step))
        def _():
            left_copy(step).wait_send()

    for from_chip in range(chips):

        @pl.when(from_chip != chip)
        def _():
            for offset in range(1, dp):
                w2_copy(from_chip, offset).wait_send()

        w3_copy(from_chip).wait_send()


def body(
    tokens,
    frozen_value_weight,
    adapter_down_weight,
    adapter_up_weight,
    output_gradient,
    adapter_per_block,
    block_live_count,
):
    dp, fsdp = lax.axis_size("dp"), lax.axis_size("fsdp")
    count_dev, model_width = tokens.shape
    width = output_gradient.shape[1]
    per_dev = adapter_per_block.shape[0]
    block_rows = count_dev // per_dev
    own, features, rank = adapter_down_weight.shape
    outputs = adapter_up_weight.shape[2]
    piece_width = features + outputs
    chunks = rank // rows_chunk
    steps = chunks - 1 + piece_width // lane_tile(piece_width)
    chips = fsdp // cores
    share_rows = frozen_value_weight.shape[0] // dp
    down, up = adapter_down_weight.transpose(0, 2, 1), adapter_up_weight
    if outputs % 128:
        down = jnp.concatenate([down, up], axis=2)
    weight = frozen_value_weight.reshape(dp, share_rows, width)
    block_group = per_dev * rows_chunk
    lanes = fsdp * block_group
    total_rows = dp * own * rows_chunk
    bf16, f32 = jnp.bfloat16, jnp.float32
    anywhere = pl.BlockSpec(memory_space=pl.ANY)
    scalars = pl.BlockSpec(memory_space=pltpu.SMEM)
    dma = pltpu.SemaphoreType.DMA
    scratch = [
        pltpu.VMEM((count_dev, model_width), bf16),
        pltpu.VMEM((count_dev, width), bf16),
        pltpu.VMEM((fsdp, count_dev, outputs), bf16),
        pltpu.VMEM((chunks, dp, own, rows_chunk, piece_width), bf16),
        pltpu.VMEM((chunks, fsdp, block_group, piece_width), bf16),
        pltpu.VMEM((chunks, fsdp, block_group, piece_width), bf16),
        pltpu.VMEM((chunks, fsdp, block_group, piece_width), bf16),
        pltpu.VMEM((chunks, dp, own, rows_chunk, piece_width), bf16),
        pltpu.VMEM((fsdp, dp, share_rows, width), bf16),
        pltpu.VMEM((fsdp, 8, lanes), jnp.int32),
        pltpu.VMEM((lanes, total_rows), bf16),
        pltpu.VMEM((total_rows, lanes), bf16),
        pltpu.VMEM((chunks, per_dev, rows_chunk, block_rows), bf16),
        pltpu.VMEM((chunks, per_dev, rows_chunk, block_rows), bf16),
        pltpu.VMEM((per_dev, block_rows, rank), bf16),
        pltpu.VMEM((per_dev, block_rows, rank), bf16),
        pltpu.VMEM((per_dev, rank, width), bf16),
        pltpu.VMEM((count_dev, width), f32),
        dma((3,)),
        dma((2, chunks)),
        dma((chunks, dp)), dma((chunks, dp)),
        dma((fsdp,)), dma((fsdp,)),
        dma((chunks, fsdp)), dma((chunks, fsdp)),
        dma((steps, fsdp)), dma((steps, fsdp)),
        dma((steps, dp)), dma((steps, dp)),
        dma((chips,)), dma((chips,)),
        dma((chips,)), dma((chips,)),
        dma((chips, dp)), dma((chips, dp)),
        dma((chips,)), dma((chips,)),
    ]
    values, input_gradient, grad_down, grad_up = pl.pallas_call(
        functools.partial(kernel, dp, fsdp),
        out_shape=(
            pltpu.VMEM((count_dev, width), bf16),
            pltpu.VMEM((count_dev, model_width), bf16),
            pltpu.VMEM((own, rank, features), f32),
            pltpu.VMEM((own, rank, outputs), f32),
        ),
        in_specs=[scalars, scalars] + [anywhere] * 5,
        out_specs=(pl.BlockSpec(memory_space=pltpu.VMEM),) * 4,
        scratch_shapes=scratch,
        compiler_params=pltpu.CompilerParams(
            collective_id=0, has_side_effects=True, vmem_limit_bytes=54_000_000
        ),
        name="lora",
    )(adapter_per_block, block_live_count, down, up, weight, tokens, output_gradient)
    return values, input_gradient, grad_down.transpose(0, 2, 1), grad_up


def solution(mesh):
    placed = (
        P(("dp", "fsdp"), None),
        P("fsdp", None),
        P("dp", "fsdp", None),
        P("dp", None, "fsdp"),
        P(("dp", "fsdp"), None),
        P(("dp", "fsdp")),
        P(("dp", "fsdp")),
    )
    return jax.shard_map(
        body,
        mesh=mesh,
        in_specs=placed,
        out_specs=(
            P(("dp", "fsdp"), None),
            P(("dp", "fsdp"), None),
            P("dp", "fsdp", None),
            P("dp", None, "fsdp"),
        ),
        check_vma=False,
    )
```

```python
import functools

import jax
import jax.numpy as jnp
from jax import lax
from jax.experimental import pallas as pl
from jax.experimental.pallas import tpu as pltpu
from jax.sharding import PartitionSpec as P

adapter_scale = 0.5
cores = 2
rows_chunk = 16
split_chunks = 2
mesh_ids = pl.DeviceIdType.MESH


def dot(left, right, left_dim, right_dim):
    return lax.dot_general(
        left, right, (((left_dim,), (right_dim,)), ((), ())), preferred_element_type=jnp.float32
    )


def partner(position, offset, size):
    if size & (size - 1):
        return lax.rem(position + offset, size)
    bit = 1
    while bit < size:
        if offset & bit:
            position = position + bit - 2 * bit * lax.rem(position // bit, 2)
        bit *= 2
    return position


def lane_tile(piece_width):
    return 384 if piece_width % 384 == 0 else piece_width


def kernel(
    dp, fsdp,
    ids_ref, fill_ref, down_ref, up_ref, w_ref, x_hbm, dy_hbm,
    y_out, dx_out, down_out, up_out,
    x, dy, dy_slices, catalog, outgoing, arrived, returned, sums_in, frozen, id_rows,
    pick, put, u_rows, v_rows, u_cols, v_cols, up_blocks, total,
    load_sem, own_sem, s1_send, s1_recv, id_send, id_recv, p_send, p_recv, t_send, t_recv,
    g_send, g_recv, right_send, right_recv, left_send, left_recv, w2_send, w2_recv, w3_send, w3_recv,
):
    my_dp, me = lax.axis_index("dp"), lax.axis_index("fsdp")
    chunks, _, own, _, piece_width = catalog.shape
    per_dev, rank_rows, block_rows = u_rows.shape[1:]
    count_dev, model_width = x.shape
    width = dy.shape[1]
    features, outputs = model_width // fsdp, width // fsdp
    block_group = per_dev * rank_rows
    lanes = fsdp * block_group
    total_rows = dp * own * rank_rows
    chips = fsdp // cores
    chip, core = me // cores, lax.rem(me, cores)
    tile_lanes = lane_tile(piece_width)
    parts = piece_width // tile_lanes
    last = chunks - 1
    whole = max(chunks - split_chunks, 0)

    def peer(offset):
        return lax.rem(me + offset, fsdp)

    def column(slice_index):
        return pl.ds(pl.multiple_of(slice_index * features, features), features)

    loads = [
        pltpu.make_async_copy(x_hbm, x, load_sem.at[0]),
        pltpu.make_async_copy(dy_hbm, dy, load_sem.at[1]),
        pltpu.make_async_copy(w_ref, frozen.at[me], load_sem.at[2]),
    ]
    owns = []
    for k in range(chunks):
        ranks = pl.ds(k * rank_rows, rank_rows)
        place = catalog.at[k, my_dp]
        if outputs % 128 == 0:
            owns.append((
                pltpu.make_async_copy(
                    down_ref.at[:, ranks, :], place.at[:, :, pl.ds(0, features)], own_sem.at[0, k]
                ),
                pltpu.make_async_copy(
                    up_ref.at[:, ranks, :], place.at[:, :, pl.ds(features, outputs)], own_sem.at[1, k]
                ),
            ))
        else:
            owns.append((pltpu.make_async_copy(down_ref.at[:, ranks, :], place, own_sem.at[0, k]),))
    for copies in owns:
        for copy in copies:
            copy.start()

    lane_block = lax.shift_right_logical(
        lax.broadcasted_iota(jnp.int32, (8, lanes), 1), rank_rows.bit_length() - 1
    )
    mine = jnp.zeros((8, lanes), jnp.int32)
    for block in range(per_dev):
        mine = jnp.where(lane_block == me * per_dev + block, ids_ref[block] + 1, mine)
    id_rows[me] = mine

    barrier = pltpu.get_barrier_semaphore()

    @pl.loop(1, fsdp)
    def _(offset):
        pl.semaphore_signal(barrier, inc=1, device_id=(my_dp, peer(offset)), device_id_type=mesh_ids)

    for offset in range(1, dp):
        pl.semaphore_signal(
            barrier, inc=1, device_id=(partner(my_dp, offset, dp), me), device_id_type=mesh_ids
        )
    pl.semaphore_wait(barrier, fsdp + dp - 2)

    def remote(source, target, send, recv, device):
        return pltpu.make_async_remote_copy(
            src_ref=source, dst_ref=target, send_sem=send, recv_sem=recv,
            device_id=device, device_id_type=mesh_ids,
        )

    def wait_group(array, semaphore):
        pltpu.make_async_copy(array, array, semaphore).wait()

    others, dp_others = pl.ds(0, fsdp - 1), pl.ds(0, dp - 1)

    def id_group():
        return id_rows.at[others]

    def s1_group(k):
        return catalog.at[k, dp_others]

    def p_group(k):
        return arrived.at[k, others]

    def t_group(k, part):
        return returned.at[k, others, :, lanes_of(k, part)]

    def g_group(k, part):
        return sums_in.at[k, dp_others, :, :, lanes_of(k, part)]

    def w2_group():
        return frozen.at[0, dp_others]

    def id_copy(offset):
        return remote(
            id_rows.at[me], id_rows.at[me], id_send, id_recv,
            (my_dp, peer(offset)),
        )

    def s1_copy(k, offset):
        return remote(
            catalog.at[k, my_dp], catalog.at[k, my_dp], s1_send.at[k], s1_recv.at[k],
            (partner(my_dp, offset, dp), me),
        )

    def p_copy(k, offset):
        return remote(
            outgoing.at[k, peer(offset)], arrived.at[k, me], p_send.at[k],
            p_recv.at[k], (my_dp, peer(offset)),
        )

    def lanes_of(k, part):
        return pl.ds(0, piece_width) if k < whole else pl.ds(part * tile_lanes, tile_lanes)

    def slot_of(k, part):
        return k if k < whole else whole + (k - whole) * parts + part

    def t_copy(k, offset, part=0):
        sent = lanes_of(k, part)
        return remote(
            outgoing.at[k, peer(offset), :, sent], returned.at[k, me, :, sent],
            t_send.at[slot_of(k, part)], t_recv.at[slot_of(k, part)], (my_dp, peer(offset)),
        )

    def g_copy(k, offset, part=0):
        other = partner(my_dp, offset, dp)
        sent = lanes_of(k, part)
        return remote(
            catalog.at[k, other, :, :, sent], sums_in.at[k, my_dp, :, :, sent],
            g_send.at[slot_of(k, part)], g_recv.at[slot_of(k, part)], (other, me),
        )

    def parts_of(k):
        return range(parts) if k >= whole else range(1)

    def right_copy(step):
        source = w_ref.at[my_dp] if step == 0 else frozen.at[me - cores * step, my_dp]
        return remote(
            source, frozen.at[me - cores * step, my_dp], right_send.at[step], right_recv.at[step],
            (my_dp, me + cores),
        )

    def left_copy(step):
        source = w_ref.at[my_dp] if step == 0 else frozen.at[me + cores * step, my_dp]
        return remote(
            source, frozen.at[me + cores * step, my_dp], left_send.at[step], left_recv.at[step],
            (my_dp, me - cores),
        )

    def sends_right(step):
        return (chip >= step) & (chip + 1 < chips)

    def sends_left(step):
        return (chip + step < chips) & (chip >= 1)

    def gets_right(step):
        return chip >= step + 1

    def gets_left(step):
        return chip + step + 1 < chips

    def w2_copy(from_chip, offset):
        row = from_chip * cores + core
        return remote(
            frozen.at[row, my_dp], frozen.at[row, my_dp], w2_send.at[from_chip],
            w2_recv.at[from_chip], (partner(my_dp, offset, dp), me),
        )

    def w3_copy(from_chip):
        row = from_chip * cores + core
        return remote(
            frozen.at[row], frozen.at[row], w3_send.at[from_chip], w3_recv.at[from_chip],
            (my_dp, me + 1 - 2 * core),
        )

    def relay(step):
        @pl.when(gets_right(step))
        def _():
            right_copy(step).wait_recv()

        @pl.when(gets_left(step))
        def _():
            left_copy(step).wait_recv()

        if step + 1 < chips - 1:

            @pl.when(sends_right(step + 1))
            def _():
                right_copy(step + 1).start()

            @pl.when(sends_left(step + 1))
            def _():
                left_copy(step + 1).start()

    def spread_shares(step):
        @pl.when(gets_right(step))
        def _():
            for offset in range(1, dp):
                w2_copy(chip - step - 1, offset).start()

        @pl.when(gets_left(step))
        def _():
            for offset in range(1, dp):
                w2_copy(chip + step + 1, offset).start()

    @pl.loop(1, fsdp)
    def _(offset):
        id_copy(offset).start()

    def share_catalog(k):
        for copy in owns[k]:
            copy.wait()
        for offset in range(1, dp):
            s1_copy(k, offset).start()

    share_catalog(0)

    @pl.when(sends_right(0))
    def _():
        right_copy(0).start()

    @pl.when(sends_left(0))
    def _():
        left_copy(0).start()

    for k in range(1, chunks):
        share_catalog(k)
    for copy in loads:
        copy.start()

    wait_group(id_group(), id_recv)

    numbers = id_rows[0]
    for position in range(1, fsdp):
        numbers = numbers + id_rows[position]
    numbers = numbers[0:1, :] - 1
    shift = rank_rows.bit_length() - 1
    row = lax.broadcasted_iota(jnp.int32, (total_rows, lanes), 0)
    lane = lax.broadcasted_iota(jnp.int32, (total_rows, lanes), 1)
    same_rank = (row & (rank_rows - 1)) == (lane & (rank_rows - 1))
    same_adapter = lax.shift_right_logical(row, shift) == numbers
    hot = jnp.where(same_rank & same_adapter, 1.0, 0.0)
    put[...] = hot.astype(jnp.bfloat16)
    pick[...] = hot.T.astype(jnp.bfloat16)

    def choose(k):
        wait_group(s1_group(k), s1_recv.at[k])
        for start in range(0, piece_width, tile_lanes):
            table = catalog[k, :, :, :, start : start + tile_lanes].reshape(total_rows, tile_lanes)
            chosen = dot(pick[...], table, 1, 0).astype(jnp.bfloat16)
            outgoing[k, :, :, start : start + tile_lanes] = chosen.reshape(
                fsdp, block_group, tile_lanes
            )
        arrived[k, me] = outgoing[k, me]

        @pl.loop(1, fsdp)
        def _(offset):
            p_copy(k, offset).start()

    def low_rank(k):
        wait_group(p_group(k), p_recv.at[k])

        zero = jnp.zeros((rank_rows, block_rows), jnp.float32)

        def gather_low(index, sums):
            result = []
            for block in range(per_dev):
                tokens = slice(block * block_rows, (block + 1) * block_rows)
                ranks = slice(block * rank_rows, (block + 1) * rank_rows)
                u = dot(arrived[k, index, ranks, :features], x[tokens, column(index)], 1, 1)
                v = dot(arrived[k, index, ranks, features:], dy_slices[index, tokens, :], 1, 1)
                result += [sums[2 * block] + u, sums[2 * block + 1] + v]
            return tuple(result)

        sums = lax.fori_loop(0, fsdp, gather_low, (zero,) * (2 * per_dev))
        token = lax.broadcasted_iota(jnp.int32, (rank_rows, block_rows), 1)
        for block in range(per_dev):
            live = (token < fill_ref[block]).astype(jnp.float32)
            u_rows[k, block] = (sums[2 * block] * live).astype(jnp.bfloat16)
            v_rows[k, block] = (sums[2 * block + 1] * live).astype(jnp.bfloat16)

        def terms_of(index):
            for block in range(per_dev):
                tokens = slice(block * block_rows, (block + 1) * block_rows)
                ranks = slice(block * rank_rows, (block + 1) * rank_rows)
                down = dot(v_rows[k, block], x[tokens, column(index)], 1, 0)
                up = dot(u_rows[k, block], dy_slices[index, tokens, :], 1, 0)
                outgoing[k, index, ranks, :features] = down.astype(jnp.bfloat16)
                outgoing[k, index, ranks, features:] = up.astype(jnp.bfloat16)

        wait_group(p_group(k), p_send.at[k])

        @pl.loop(1, fsdp)
        def _(offset):
            terms_of(peer(offset))
            if k < whole:

                @pl.when(offset > 1)
                def _():
                    t_copy(k, offset - 1).start()

        terms_of(me)
        if k < whole:
            t_copy(k, fsdp - 1).start()
        elif k < last:
            for part in parts_of(k):

                @pl.loop(1, fsdp)
                def _(offset):
                    t_copy(k, offset, part).start()

        returned[k, me] = outgoing[k, me]

    def send_last(part):
        slot = slot_of(last - 1, part)
        wait_group(t_group(last - 1, part), t_send.at[slot])

        @pl.loop(1, fsdp)
        def _(offset):
            t_copy(last, offset, part).start()

    def combine(k, part=0):
        if part == 0:
            wait_group(s1_group(k), s1_send.at[k])

        wait_group(t_group(k, part), t_recv.at[slot_of(k, part)])

        starts = [part * tile_lanes] if k >= whole else range(0, piece_width, tile_lanes)
        for start in starts:
            tile = slice(start, start + tile_lanes)
            terms = returned[k, :, :, tile].reshape(lanes, tile_lanes)
            added = dot(put[...], terms, 1, 0).astype(jnp.bfloat16)
            catalog[k, :, :, :, tile] = added.reshape(dp, own, rank_rows, tile_lanes)
        for offset in range(1, dp):
            g_copy(k, offset, part).start()
        for start in starts:
            tile = slice(start, start + tile_lanes)
            sums_in[k, my_dp, :, :, tile] = catalog[k, my_dp, :, :, tile]

    def finish(k):
        for part in parts_of(k):
            wait_group(g_group(k, part), g_recv.at[slot_of(k, part)])
        added = sums_in[k, 0].astype(jnp.float32)
        for position in range(1, dp):
            added = added + sums_in[k, position].astype(jnp.float32)
        added = adapter_scale * added
        ranks = slice(k * rank_rows, (k + 1) * rank_rows)
        down_out[:, ranks, :] = added[:, :, :features]
        up_out[:, ranks, :] = added[:, :, features:]

    def columns_of_low():
        for block in range(per_dev):
            for rows, columns in ((u_rows, u_cols), (v_rows, v_cols)):
                whole = jnp.concatenate([rows[k, block] for k in range(chunks)], axis=0)
                columns[block] = whole.astype(jnp.float32).T.astype(jnp.bfloat16)
            for index in range(fsdp):
                part = slice(index * outputs, (index + 1) * outputs)
                ranks = slice(block * rank_rows, (block + 1) * rank_rows)
                for k in range(chunks):
                    up_blocks[block, k * rank_rows : (k + 1) * rank_rows, part] = arrived[
                        k, index, ranks, features:
                    ]

    def base_values():
        @pl.loop(0, fsdp)
        def _(index):
            product = dot(x[:, column(index)], frozen[index].reshape(features, width), 1, 0)

            @pl.when(index == 0)
            def _():
                total[...] = product

            @pl.when(index > 0)
            def _():
                total[...] += product

    def base_grads(first, end):
        @pl.loop(first, end)
        def _(index):
            base_grad = dot(dy[...], frozen[index].reshape(features, width), 1, 1)
            for block in range(per_dev):
                tokens = slice(block * block_rows, (block + 1) * block_rows)
                ranks = slice(block * rank_rows, (block + 1) * rank_rows)
                down = jnp.concatenate(
                    [arrived[k, index, ranks, :features] for k in range(chunks)], axis=0
                )
                pulled = dot(v_cols[block], down, 1, 0).astype(jnp.bfloat16).astype(jnp.float32)
                mixed = base_grad[tokens, :] + adapter_scale * pulled
                dx_out[tokens, column(index)] = mixed.astype(jnp.bfloat16)

    def last_values():
        for block in range(per_dev):
            tokens = slice(block * block_rows, (block + 1) * block_rows)
            lifted = dot(u_cols[block], up_blocks[block], 1, 0)
            lifted = lifted.astype(jnp.bfloat16).astype(jnp.float32)
            y_out[tokens, :] = (total[tokens, :] + adapter_scale * lifted).astype(jnp.bfloat16)

    def pass_core(step):
        def give(from_chip):
            wait_group(w2_group(), w2_recv.at[from_chip])
            w3_copy(from_chip).start()

        @pl.when(gets_right(step))
        def _():
            give(chip - step - 1)

        @pl.when(gets_left(step))
        def _():
            give(chip + step + 1)

    hops = chips - 1
    relay(0)
    choose(0)
    spread_shares(0)
    for copy in loads:
        copy.wait()
    w3_copy(chip).start()
    for index in range(fsdp):
        dy_slices[index] = dy[:, index * outputs : (index + 1) * outputs]
    choose(1)
    low_rank(0)
    for step in range(1, hops):
        relay(step)
        spread_shares(step)
    choose(2)
    low_rank(1)
    pass_core(0)
    for k in range(3, chunks):
        choose(k)
        combine(k - 3)
        low_rank(k - 1)
    for step in range(1, hops):
        pass_core(step)
    for from_chip in range(chips):
        w3_copy(from_chip).wait_recv()
    base_values()
    combine(chunks - 3)
    low_rank(last)
    columns_of_low()
    order = [(k, part) for k in (last - 1, last) for part in parts_of(k)]
    count, early = len(order), len(parts_of(last))
    share = max(fsdp // 4, 1)
    for position, (k, part) in enumerate(order):
        if position < early:
            send_last(part)
        if position == 0:
            base_grads(0, share)
        if position == early:
            base_grads(share, 2 * share)
        combine(k, part)
    base_grads(2 * share, fsdp)
    last_values()
    for k in range(chunks):
        finish(k)

    def drain():
        wait_group(id_group(), id_send)
        for k in range(chunks):
            for part in parts_of(k):
                slot = slot_of(k, part)
                if k != last - 1:
                    wait_group(t_group(k, part), t_send.at[slot])
                wait_group(g_group(k, part), g_send.at[slot])
        for step in range(hops):

            @pl.when(sends_right(step))
            def _():
                right_copy(step).wait_send()

            @pl.when(sends_left(step))
            def _():
                left_copy(step).wait_send()

        for from_chip in range(chips):

            @pl.when(from_chip != chip)
            def _():
                wait_group(w2_group(), w2_send.at[from_chip])

            w3_copy(from_chip).wait_send()

    drain()


def body(
    tokens,
    frozen_value_weight,
    adapter_down_weight,
    adapter_up_weight,
    output_gradient,
    adapter_per_block,
    block_live_count,
):
    dp, fsdp = lax.axis_size("dp"), lax.axis_size("fsdp")
    count_dev, model_width = tokens.shape
    width = output_gradient.shape[1]
    per_dev = adapter_per_block.shape[0]
    block_rows = count_dev // per_dev
    own, features, rank = adapter_down_weight.shape
    outputs = adapter_up_weight.shape[2]
    piece_width = features + outputs
    chunks = rank // rows_chunk
    split = min(split_chunks, chunks)
    steps = chunks - split + split * (piece_width // lane_tile(piece_width))
    chips = fsdp // cores
    share_rows = frozen_value_weight.shape[0] // dp
    down, up = adapter_down_weight.transpose(0, 2, 1), adapter_up_weight
    if outputs % 128:
        down = jnp.concatenate([down, up], axis=2)
    weight = frozen_value_weight.reshape(dp, share_rows, width)
    block_group = per_dev * rows_chunk
    lanes = fsdp * block_group
    total_rows = dp * own * rows_chunk
    bf16, f32 = jnp.bfloat16, jnp.float32
    anywhere = pl.BlockSpec(memory_space=pl.ANY)
    scalars = pl.BlockSpec(memory_space=pltpu.SMEM)
    dma = pltpu.SemaphoreType.DMA
    scratch = [
        pltpu.VMEM((count_dev, model_width), bf16),
        pltpu.VMEM((count_dev, width), bf16),
        pltpu.VMEM((fsdp, count_dev, outputs), bf16),
        pltpu.VMEM((chunks, dp, own, rows_chunk, piece_width), bf16),
        pltpu.VMEM((chunks, fsdp, block_group, piece_width), bf16),
        pltpu.VMEM((chunks, fsdp, block_group, piece_width), bf16),
        pltpu.VMEM((chunks, fsdp, block_group, piece_width), bf16),
        pltpu.VMEM((chunks, dp, own, rows_chunk, piece_width), bf16),
        pltpu.VMEM((fsdp, dp, share_rows, width), bf16),
        pltpu.VMEM((fsdp, 8, lanes), jnp.int32),
        pltpu.VMEM((lanes, total_rows), bf16),
        pltpu.VMEM((total_rows, lanes), bf16),
        pltpu.VMEM((chunks, per_dev, rows_chunk, block_rows), bf16),
        pltpu.VMEM((chunks, per_dev, rows_chunk, block_rows), bf16),
        pltpu.VMEM((per_dev, block_rows, rank), bf16),
        pltpu.VMEM((per_dev, block_rows, rank), bf16),
        pltpu.VMEM((per_dev, rank, width), bf16),
        pltpu.VMEM((count_dev, width), f32),
        dma((3,)),
        dma((2, chunks)),
        dma((chunks,)), dma((chunks,)),
        dma, dma,
        dma((chunks,)), dma((chunks,)),
        dma((steps,)), dma((steps,)),
        dma((steps,)), dma((steps,)),
        dma((chips - 1,)), dma((chips - 1,)),
        dma((chips - 1,)), dma((chips - 1,)),
        dma((chips,)), dma((chips,)),
        dma((chips,)), dma((chips,)),
    ]
    values, input_gradient, grad_down, grad_up = pl.pallas_call(
        functools.partial(kernel, dp, fsdp),
        out_shape=(
            pltpu.VMEM((count_dev, width), bf16),
            pltpu.VMEM((count_dev, model_width), bf16),
            pltpu.VMEM((own, rank, features), f32),
            pltpu.VMEM((own, rank, outputs), f32),
        ),
        in_specs=[scalars, scalars] + [anywhere] * 5,
        out_specs=(pl.BlockSpec(memory_space=pltpu.VMEM),) * 4,
        scratch_shapes=scratch,
        compiler_params=pltpu.CompilerParams(
            collective_id=0, has_side_effects=True, vmem_limit_bytes=54_000_000
        ),
        name="lora",
    )(adapter_per_block, block_live_count, down, up, weight, tokens, output_gradient)
    return values, input_gradient, grad_down.transpose(0, 2, 1), grad_up


def solution(mesh):
    placed = (
        P(("dp", "fsdp"), None),
        P("fsdp", None),
        P("dp", "fsdp", None),
        P("dp", None, "fsdp"),
        P(("dp", "fsdp"), None),
        P(("dp", "fsdp")),
        P(("dp", "fsdp")),
    )
    return jax.shard_map(
        body,
        mesh=mesh,
        in_specs=placed,
        out_specs=(
            P(("dp", "fsdp"), None),
            P(("dp", "fsdp"), None),
            P("dp", "fsdp", None),
            P("dp", None, "fsdp"),
        ),
        check_vma=False,
    )
```

```python
import functools

import jax
import jax.numpy as jnp
from jax import lax
from jax.experimental import pallas as pl
from jax.experimental.pallas import tpu as pltpu
from jax.sharding import PartitionSpec as P

adapter_scale = 0.5
cores = 2
rows_chunk = 16
split_chunks = 2
cross_chunks = 1
mesh_ids = pl.DeviceIdType.MESH


def dot(left, right, left_dim, right_dim):
    return lax.dot_general(
        left, right, (((left_dim,), (right_dim,)), ((), ())), preferred_element_type=jnp.float32
    )


def partner(position, offset, size):
    if size & (size - 1):
        return lax.rem(position + offset, size)
    bit = 1
    while bit < size:
        if offset & bit:
            position = position + bit - 2 * bit * lax.rem(position // bit, 2)
        bit *= 2
    return position


def lane_tile(piece_width):
    return 384 if piece_width % 384 == 0 else piece_width


def crossing_chunks(chunks, chips):
    return min(cross_chunks, chunks - 2) if chips % 2 == 0 else 0


def kernel(
    dp, fsdp,
    ids_ref, fill_ref, down_ref, up_ref, w_ref, x_hbm, dy_hbm,
    y_out, dx_out, down_out, up_out,
    x, dy, dy_slices, catalog, outgoing, arrived, returned, sums_in, frozen, id_rows,
    pick, put, u_rows, v_rows, u_cols, v_cols, up_blocks, total,
    load_sem, own_sem, s1_send, s1_recv, id_send, id_recv, p_send, p_recv, t_send, t_recv,
    g_send, g_recv, right_send, right_recv, left_send, left_recv, w2_send, w2_recv, relay_recv,
    x_send, x_recv, c_send, c_recv, crossed, w3_send, w3_recv,
):
    my_dp, me = lax.axis_index("dp"), lax.axis_index("fsdp")
    chunks, _, own, _, piece_width = catalog.shape
    per_dev, rank_rows, block_rows = u_rows.shape[1:]
    count_dev, model_width = x.shape
    width = dy.shape[1]
    features, outputs = model_width // fsdp, width // fsdp
    block_group = per_dev * rank_rows
    lanes = fsdp * block_group
    total_rows = dp * own * rank_rows
    chips = fsdp // cores
    chip, core = me // cores, lax.rem(me, cores)
    tile_lanes = lane_tile(piece_width)
    parts = piece_width // tile_lanes
    crossing = crossing_chunks(chunks, chips)
    direct = chunks - crossing
    half = fsdp // 2
    first = me // half * half
    local, across = me - first, lax.rem(me + half, fsdp)
    two_hops = dp == 4
    share_half = frozen.shape[2] // 2
    last = chunks - 1
    whole = max(chunks - split_chunks, 0)

    def peer(offset):
        return lax.rem(me + offset, fsdp)

    def column(slice_index):
        return pl.ds(pl.multiple_of(slice_index * features, features), features)

    loads = [
        pltpu.make_async_copy(x_hbm, x, load_sem.at[0]),
        pltpu.make_async_copy(dy_hbm, dy, load_sem.at[1]),
        pltpu.make_async_copy(w_ref, frozen.at[me], load_sem.at[2]),
    ]
    owns = []
    for k in range(chunks):
        ranks = pl.ds(k * rank_rows, rank_rows)
        place = catalog.at[k, my_dp]
        if outputs % 128 == 0:
            owns.append((
                pltpu.make_async_copy(
                    down_ref.at[:, ranks, :], place.at[:, :, pl.ds(0, features)], own_sem.at[0, k]
                ),
                pltpu.make_async_copy(
                    up_ref.at[:, ranks, :], place.at[:, :, pl.ds(features, outputs)], own_sem.at[1, k]
                ),
            ))
        else:
            owns.append((pltpu.make_async_copy(down_ref.at[:, ranks, :], place, own_sem.at[0, k]),))
    for copies in owns:
        for copy in copies:
            copy.start()

    lane_block = lax.shift_right_logical(
        lax.broadcasted_iota(jnp.int32, (8, lanes), 1), rank_rows.bit_length() - 1
    )
    mine = jnp.zeros((8, lanes), jnp.int32)
    for block in range(per_dev):
        mine = jnp.where(lane_block == me * per_dev + block, ids_ref[block] + 1, mine)
    id_rows[me] = mine

    barrier = pltpu.get_barrier_semaphore()

    @pl.loop(1, fsdp)
    def _(offset):
        pl.semaphore_signal(barrier, inc=1, device_id=(my_dp, peer(offset)), device_id_type=mesh_ids)

    for offset in range(1, dp):
        pl.semaphore_signal(
            barrier, inc=1, device_id=(partner(my_dp, offset, dp), me), device_id_type=mesh_ids
        )
    pl.semaphore_wait(barrier, fsdp + dp - 2)

    def remote(source, target, send, recv, device):
        return pltpu.make_async_remote_copy(
            src_ref=source, dst_ref=target, send_sem=send, recv_sem=recv,
            device_id=device, device_id_type=mesh_ids,
        )

    def wait_group(array, semaphore):
        pltpu.make_async_copy(array, array, semaphore).wait()

    others, dp_others = pl.ds(0, fsdp - 1), pl.ds(0, dp - 1)

    def id_group():
        return id_rows.at[others]

    def s1_group(k):
        return catalog.at[k, dp_others]

    def p_group(k):
        return arrived.at[k, others] if k < direct else arrived.at[k, pl.ds(0, fsdp - 2)]

    def t_group(k, part):
        return returned.at[k, others, :, lanes_of(k, part)]

    def g_group(k, part):
        return sums_in.at[k, dp_others, :, :, lanes_of(k, part)]

    def w2_group(shares=dp - 1):
        return frozen.at[0, pl.ds(0, shares)]

    def id_copy(offset):
        return remote(
            id_rows.at[me], id_rows.at[me], id_send, id_recv,
            (my_dp, peer(offset)),
        )

    def s1_copy(k, offset):
        return remote(
            catalog.at[k, my_dp], catalog.at[k, my_dp], s1_send.at[k], s1_recv.at[k],
            (partner(my_dp, offset, dp), me),
        )

    def p_copy(k, offset):
        return remote(
            outgoing.at[k, peer(offset)], arrived.at[k, me], p_send.at[k],
            p_recv.at[k], (my_dp, peer(offset)),
        )

    def lanes_of(k, part):
        return pl.ds(0, piece_width) if k < whole else pl.ds(part * tile_lanes, tile_lanes)

    def slot_of(k, part):
        return k if k < whole else whole + (k - whole) * parts + part

    def half_copies(k, offset):
        target = lax.rem(local + offset, half)
        return [
            remote(
                outgoing.at[k, slot * half + target], arrived.at[k, place], p_send.at[k], p_recv.at[k],
                (my_dp, first + target),
            )
            for slot, place in enumerate((me, across))
        ]

    def cross_copy(k):
        return remote(
            catalog.at[k, my_dp], crossed.at[k - direct, my_dp], x_send.at[k - direct],
            x_recv.at[k - direct], (my_dp, across),
        )

    def crossed_copy(k, offset):
        return remote(
            crossed.at[k - direct, my_dp], crossed.at[k - direct, my_dp], c_send.at[k - direct],
            c_recv.at[k - direct], (partner(my_dp, offset, dp), me),
        )

    def spread_crossed(k):
        cross_copy(k).wait_recv()
        for offset in range(1, dp):
            crossed_copy(k, offset).start()

    def t_copy(k, offset, part=0):
        sent = lanes_of(k, part)
        return remote(
            outgoing.at[k, peer(offset), :, sent], returned.at[k, me, :, sent],
            t_send.at[slot_of(k, part)], t_recv.at[slot_of(k, part)], (my_dp, peer(offset)),
        )

    def g_copy(k, offset, part=0):
        other = partner(my_dp, offset, dp)
        sent = lanes_of(k, part)
        return remote(
            catalog.at[k, other, :, :, sent], sums_in.at[k, my_dp, :, :, sent],
            g_send.at[slot_of(k, part)], g_recv.at[slot_of(k, part)], (other, me),
        )

    def parts_of(k):
        return range(parts) if k >= whole else range(1)

    def right_copy(step):
        source = w_ref.at[my_dp] if step == 0 else frozen.at[me - cores * step, my_dp]
        return remote(
            source, frozen.at[me - cores * step, my_dp], right_send.at[step], right_recv.at[step],
            (my_dp, me + cores),
        )

    def left_copy(step):
        source = w_ref.at[my_dp] if step == 0 else frozen.at[me + cores * step, my_dp]
        return remote(
            source, frozen.at[me + cores * step, my_dp], left_send.at[step], left_recv.at[step],
            (my_dp, me - cores),
        )

    def sends_right(step):
        return (chip >= step) & (chip + 1 < chips)

    def sends_left(step):
        return (chip + step < chips) & (chip >= 1)

    def gets_right(step):
        return chip >= step + 1

    def gets_left(step):
        return chip + step + 1 < chips

    def w2_copy(from_chip, offset):
        row = from_chip * cores + core
        return remote(
            frozen.at[row, my_dp], frozen.at[row, my_dp], w2_send.at[from_chip],
            w2_recv.at[from_chip], (partner(my_dp, offset, dp), me),
        )

    def w3_copy(from_chip):
        row = from_chip * cores + core
        return remote(
            frozen.at[row], frozen.at[row], w3_send.at[from_chip], w3_recv.at[from_chip],
            (my_dp, me + 1 - 2 * core),
        )

    def relay(step):
        @pl.when(gets_right(step))
        def _():
            right_copy(step).wait_recv()

        @pl.when(gets_left(step))
        def _():
            left_copy(step).wait_recv()

        if step + 1 < chips - 1:

            @pl.when(sends_right(step + 1))
            def _():
                right_copy(step + 1).start()

            @pl.when(sends_left(step + 1))
            def _():
                left_copy(step + 1).start()

    def relay_copy(from_chip, source, target, part):
        row = from_chip * cores + core
        rows = frozen.at[row, partner(my_dp, source, dp), pl.ds(part * share_half, share_half)]
        return remote(
            rows, rows, w2_send.at[from_chip], relay_recv.at[from_chip],
            (partner(my_dp, target, dp), me),
        )

    def each_arrived(step, action):
        @pl.when(gets_right(step))
        def _():
            action(chip - step - 1)

        @pl.when(gets_left(step))
        def _():
            action(chip + step + 1)

    def spread_shares(step):
        def send(from_chip):
            for offset in range(1, 3 if two_hops else dp):
                w2_copy(from_chip, offset).start()

        each_arrived(step, send)

    def relay_shares(step):
        def send(from_chip):
            wait_group(w2_group(2), w2_recv.at[from_chip])
            relay_copy(from_chip, 1, 2, 0).start()
            relay_copy(from_chip, 2, 1, 1).start()

        if two_hops:
            each_arrived(step, send)

    @pl.loop(1, fsdp)
    def _(offset):
        id_copy(offset).start()

    def share_catalog(k):
        for copy in owns[k]:
            copy.wait()
        for offset in range(1, dp):
            s1_copy(k, offset).start()

    share_catalog(0)

    @pl.when(sends_right(0))
    def _():
        right_copy(0).start()

    @pl.when(sends_left(0))
    def _():
        left_copy(0).start()

    for k in range(1, chunks):
        share_catalog(k)
    for copy in loads:
        copy.start()

    wait_group(id_group(), id_recv)

    numbers = id_rows[0]
    for position in range(1, fsdp):
        numbers = numbers + id_rows[position]
    numbers = numbers[0:1, :] - 1
    shift = rank_rows.bit_length() - 1
    row = lax.broadcasted_iota(jnp.int32, (total_rows, lanes), 0)
    lane = lax.broadcasted_iota(jnp.int32, (total_rows, lanes), 1)
    same_rank = (row & (rank_rows - 1)) == (lane & (rank_rows - 1))
    same_adapter = lax.shift_right_logical(row, shift) == numbers
    hot = jnp.where(same_rank & same_adapter, 1.0, 0.0)
    put[...] = hot.astype(jnp.bfloat16)
    pick[...] = hot.T.astype(jnp.bfloat16)

    def choose(k):
        wait_group(s1_group(k), s1_recv.at[k])
        tables, picked, targets = [catalog.at[k]], pick[...], fsdp
        if k >= direct:
            wait_group(s1_group(k), c_recv.at[k - direct])
            tables.append(crossed.at[k - direct])
            rows = pl.ds(pl.multiple_of(first * block_group, half * block_group), half * block_group)
            picked, targets = pick[rows, :], half
        for slot, table_ref in enumerate(tables):
            for start in range(0, piece_width, tile_lanes):
                tile = slice(start, start + tile_lanes)
                table = table_ref[:, :, :, tile].reshape(total_rows, tile_lanes)
                chosen = dot(picked, table, 1, 0).astype(jnp.bfloat16)
                outgoing[k, slot * half : slot * half + targets, :, tile] = chosen.reshape(
                    targets, block_group, tile_lanes
                )
        if k < direct:
            arrived[k, me] = outgoing[k, me]

            @pl.loop(1, fsdp)
            def _(offset):
                p_copy(k, offset).start()

        else:
            arrived[k, me] = outgoing[k, local]
            arrived[k, across] = outgoing[k, half + local]

            @pl.loop(1, half)
            def _(offset):
                for copy in half_copies(k, offset):
                    copy.start()

    def low_rank(k):
        wait_group(p_group(k), p_recv.at[k])

        zero = jnp.zeros((rank_rows, block_rows), jnp.float32)

        def gather_low(index, sums):
            result = []
            for block in range(per_dev):
                tokens = slice(block * block_rows, (block + 1) * block_rows)
                ranks = slice(block * rank_rows, (block + 1) * rank_rows)
                u = dot(arrived[k, index, ranks, :features], x[tokens, column(index)], 1, 1)
                v = dot(arrived[k, index, ranks, features:], dy_slices[index, tokens, :], 1, 1)
                result += [sums[2 * block] + u, sums[2 * block + 1] + v]
            return tuple(result)

        sums = lax.fori_loop(0, fsdp, gather_low, (zero,) * (2 * per_dev))
        token = lax.broadcasted_iota(jnp.int32, (rank_rows, block_rows), 1)
        for block in range(per_dev):
            live = (token < fill_ref[block]).astype(jnp.float32)
            u_rows[k, block] = (sums[2 * block] * live).astype(jnp.bfloat16)
            v_rows[k, block] = (sums[2 * block + 1] * live).astype(jnp.bfloat16)

        def terms_of(index):
            for block in range(per_dev):
                tokens = slice(block * block_rows, (block + 1) * block_rows)
                ranks = slice(block * rank_rows, (block + 1) * rank_rows)
                down = dot(v_rows[k, block], x[tokens, column(index)], 1, 0)
                up = dot(u_rows[k, block], dy_slices[index, tokens, :], 1, 0)
                outgoing[k, index, ranks, :features] = down.astype(jnp.bfloat16)
                outgoing[k, index, ranks, features:] = up.astype(jnp.bfloat16)

        wait_group(p_group(k), p_send.at[k])

        @pl.loop(1, fsdp)
        def _(offset):
            terms_of(peer(offset))
            if k < whole:

                @pl.when(offset > 1)
                def _():
                    t_copy(k, offset - 1).start()

        terms_of(me)
        if k < whole:
            t_copy(k, fsdp - 1).start()
        else:
            for part in parts_of(k):

                @pl.loop(1, fsdp)
                def _(offset):
                    t_copy(k, offset, part).start()

        returned[k, me] = outgoing[k, me]

    def combine(k, part=0):
        if part == 0:
            wait_group(s1_group(k), s1_send.at[k])
            if k >= direct:
                cross_copy(k).wait_send()

        wait_group(t_group(k, part), t_recv.at[slot_of(k, part)])

        starts = [part * tile_lanes] if k >= whole else range(0, piece_width, tile_lanes)
        for start in starts:
            tile = slice(start, start + tile_lanes)
            terms = returned[k, :, :, tile].reshape(lanes, tile_lanes)
            added = dot(put[...], terms, 1, 0).astype(jnp.bfloat16)
            catalog[k, :, :, :, tile] = added.reshape(dp, own, rank_rows, tile_lanes)
        for offset in range(1, dp):
            g_copy(k, offset, part).start()
        for start in starts:
            tile = slice(start, start + tile_lanes)
            sums_in[k, my_dp, :, :, tile] = catalog[k, my_dp, :, :, tile]

    def finish(k):
        for part in parts_of(k):
            wait_group(g_group(k, part), g_recv.at[slot_of(k, part)])
        added = sums_in[k, 0].astype(jnp.float32)
        for position in range(1, dp):
            added = added + sums_in[k, position].astype(jnp.float32)
        added = adapter_scale * added
        ranks = slice(k * rank_rows, (k + 1) * rank_rows)
        down_out[:, ranks, :] = added[:, :, :features]
        up_out[:, ranks, :] = added[:, :, features:]

    def columns_of_low():
        for block in range(per_dev):
            for rows, columns in ((u_rows, u_cols), (v_rows, v_cols)):
                whole = jnp.concatenate([rows[k, block] for k in range(chunks)], axis=0)
                columns[block] = whole.astype(jnp.float32).T.astype(jnp.bfloat16)
            for index in range(fsdp):
                part = slice(index * outputs, (index + 1) * outputs)
                ranks = slice(block * rank_rows, (block + 1) * rank_rows)
                for k in range(chunks):
                    up_blocks[block, k * rank_rows : (k + 1) * rank_rows, part] = arrived[
                        k, index, ranks, features:
                    ]

    def base_values(first, end):
        @pl.loop(first, end)
        def _(index):
            product = dot(x[:, column(index)], frozen[index].reshape(features, width), 1, 0)

            @pl.when(index == 0)
            def _():
                total[...] = product

            @pl.when(index > 0)
            def _():
                total[...] += product

    def base_grads(first, end):
        @pl.loop(first, end)
        def _(index):
            base_grad = dot(dy[...], frozen[index].reshape(features, width), 1, 1)
            for block in range(per_dev):
                tokens = slice(block * block_rows, (block + 1) * block_rows)
                ranks = slice(block * rank_rows, (block + 1) * rank_rows)
                down = jnp.concatenate(
                    [arrived[k, index, ranks, :features] for k in range(chunks)], axis=0
                )
                pulled = dot(v_cols[block], down, 1, 0).astype(jnp.bfloat16).astype(jnp.float32)
                mixed = base_grad[tokens, :] + adapter_scale * pulled
                dx_out[tokens, column(index)] = mixed.astype(jnp.bfloat16)

    def last_values():
        for block in range(per_dev):
            tokens = slice(block * block_rows, (block + 1) * block_rows)
            lifted = dot(u_cols[block], up_blocks[block], 1, 0)
            lifted = lifted.astype(jnp.bfloat16).astype(jnp.float32)
            y_out[tokens, :] = (total[tokens, :] + adapter_scale * lifted).astype(jnp.bfloat16)

    def pass_core(step):
        def give(from_chip):
            if two_hops:
                wait_group(w2_group(1), relay_recv.at[from_chip])
            else:
                wait_group(w2_group(), w2_recv.at[from_chip])
            w3_copy(from_chip).start()

        each_arrived(step, give)

    hops = chips - 1
    relay(0)
    for k in range(direct, chunks):
        cross_copy(k).start()
    choose(0)
    for copy in loads:
        copy.wait()
    w3_copy(chip).start()
    for index in range(fsdp):
        dy_slices[index] = dy[:, index * outputs : (index + 1) * outputs]
    choose(1)
    spread_shares(0)
    low_rank(0)
    for k in range(direct, chunks):
        spread_crossed(k)
    for step in range(1, min(2, hops)):
        relay(step)
        spread_shares(step)
    choose(2)
    low_rank(1)
    relay_shares(0)
    for k in range(3, chunks):
        choose(k)
    for step in range(2, hops):
        relay(step)
        spread_shares(step)
    relay_shares(1)
    for k in range(chunks - 3):
        combine(k)
    for step in range(2, hops):
        relay_shares(step)
    for k in range(2, last):
        low_rank(k)
    for step in range(min(2, hops)):
        pass_core(step)
    low_rank(last)
    for step in range(2, hops):
        pass_core(step)
    combine(chunks - 3)
    columns_of_low()
    for from_chip in range(chips):
        w3_copy(from_chip).wait_recv()

    order = [(k, part) for k in (last - 1, last) for part in parts_of(k)]
    middle, quarter = fsdp // 2, fsdp // 4
    fill = [(base_values, 0, middle), (base_values, middle, fsdp), (base_grads, 0, quarter)]
    fill += [(base_grads, quarter, middle)]
    for k, part in order:
        if fill:
            work, start, end = fill.pop(0)
            work(start, end)
        combine(k, part)
    for work, start, end in fill + [(base_grads, middle, fsdp)]:
        work(start, end)
    last_values()
    for k in range(chunks):
        finish(k)

    def drain():
        for k in range(direct, chunks):
            wait_group(s1_group(k), c_send.at[k - direct])
        wait_group(id_group(), id_send)
        for k in range(chunks):
            for part in parts_of(k):
                slot = slot_of(k, part)
                wait_group(t_group(k, part), t_send.at[slot])
                wait_group(g_group(k, part), g_send.at[slot])
        for step in range(hops):

            @pl.when(sends_right(step))
            def _():
                right_copy(step).wait_send()

            @pl.when(sends_left(step))
            def _():
                left_copy(step).wait_send()

        for from_chip in range(chips):

            @pl.when(from_chip != chip)
            def _():
                wait_group(w2_group(), w2_send.at[from_chip])

            w3_copy(from_chip).wait_send()

    drain()


def body(
    tokens,
    frozen_value_weight,
    adapter_down_weight,
    adapter_up_weight,
    output_gradient,
    adapter_per_block,
    block_live_count,
):
    dp, fsdp = lax.axis_size("dp"), lax.axis_size("fsdp")
    count_dev, model_width = tokens.shape
    width = output_gradient.shape[1]
    per_dev = adapter_per_block.shape[0]
    block_rows = count_dev // per_dev
    own, features, rank = adapter_down_weight.shape
    outputs = adapter_up_weight.shape[2]
    piece_width = features + outputs
    chunks = rank // rows_chunk
    split = min(split_chunks, chunks)
    steps = chunks - split + split * (piece_width // lane_tile(piece_width))
    chips = fsdp // cores
    share_rows = frozen_value_weight.shape[0] // dp
    crossing = crossing_chunks(chunks, chips)
    down, up = adapter_down_weight.transpose(0, 2, 1), adapter_up_weight
    if outputs % 128:
        down = jnp.concatenate([down, up], axis=2)
    weight = frozen_value_weight.reshape(dp, share_rows, width)
    block_group = per_dev * rows_chunk
    lanes = fsdp * block_group
    total_rows = dp * own * rows_chunk
    bf16, f32 = jnp.bfloat16, jnp.float32
    anywhere = pl.BlockSpec(memory_space=pl.ANY)
    scalars = pl.BlockSpec(memory_space=pltpu.SMEM)
    dma = pltpu.SemaphoreType.DMA
    scratch = [
        pltpu.VMEM((count_dev, model_width), bf16),
        pltpu.VMEM((count_dev, width), bf16),
        pltpu.VMEM((fsdp, count_dev, outputs), bf16),
        pltpu.VMEM((chunks, dp, own, rows_chunk, piece_width), bf16),
        pltpu.VMEM((chunks, fsdp, block_group, piece_width), bf16),
        pltpu.VMEM((chunks, fsdp, block_group, piece_width), bf16),
        pltpu.VMEM((chunks, fsdp, block_group, piece_width), bf16),
        pltpu.VMEM((chunks, dp, own, rows_chunk, piece_width), bf16),
        pltpu.VMEM((fsdp, dp, share_rows, width), bf16),
        pltpu.VMEM((fsdp, 8, lanes), jnp.int32),
        pltpu.VMEM((lanes, total_rows), bf16),
        pltpu.VMEM((total_rows, lanes), bf16),
        pltpu.VMEM((chunks, per_dev, rows_chunk, block_rows), bf16),
        pltpu.VMEM((chunks, per_dev, rows_chunk, block_rows), bf16),
        pltpu.VMEM((per_dev, block_rows, rank), bf16),
        pltpu.VMEM((per_dev, block_rows, rank), bf16),
        pltpu.VMEM((per_dev, rank, width), bf16),
        pltpu.VMEM((count_dev, width), f32),
        dma((3,)),
        dma((2, chunks)),
        dma((chunks,)), dma((chunks,)),
        dma, dma,
        dma((chunks,)), dma((chunks,)),
        dma((steps,)), dma((steps,)),
        dma((steps,)), dma((steps,)),
        dma((chips - 1,)), dma((chips - 1,)),
        dma((chips - 1,)), dma((chips - 1,)),
        dma((chips,)), dma((chips,)), dma((chips,)),
        dma((max(crossing, 1),)), dma((max(crossing, 1),)),
        dma((max(crossing, 1),)), dma((max(crossing, 1),)),
        pltpu.VMEM((max(crossing, 1), dp, own, rows_chunk, piece_width), bf16),
        dma((chips,)), dma((chips,)),
    ]
    values, input_gradient, grad_down, grad_up = pl.pallas_call(
        functools.partial(kernel, dp, fsdp),
        out_shape=(
            pltpu.VMEM((count_dev, width), bf16),
            pltpu.VMEM((count_dev, model_width), bf16),
            pltpu.VMEM((own, rank, features), f32),
            pltpu.VMEM((own, rank, outputs), f32),
        ),
        in_specs=[scalars, scalars] + [anywhere] * 5,
        out_specs=(pl.BlockSpec(memory_space=pltpu.VMEM),) * 4,
        scratch_shapes=scratch,
        compiler_params=pltpu.CompilerParams(
            collective_id=0, has_side_effects=True, vmem_limit_bytes=56_500_000
        ),
        name="lora",
    )(adapter_per_block, block_live_count, down, up, weight, tokens, output_gradient)
    return values, input_gradient, grad_down.transpose(0, 2, 1), grad_up


def solution(mesh):
    placed = (
        P(("dp", "fsdp"), None),
        P("fsdp", None),
        P("dp", "fsdp", None),
        P("dp", None, "fsdp"),
        P(("dp", "fsdp"), None),
        P(("dp", "fsdp")),
        P(("dp", "fsdp")),
    )
    return jax.shard_map(
        body,
        mesh=mesh,
        in_specs=placed,
        out_specs=(
            P(("dp", "fsdp"), None),
            P(("dp", "fsdp"), None),
            P("dp", "fsdp", None),
            P("dp", None, "fsdp"),
        ),
        check_vma=False,
    )
```

```python
import functools

import jax
import jax.numpy as jnp
from jax import lax
from jax.experimental import pallas as pl
from jax.experimental.pallas import tpu as pltpu
from jax.sharding import PartitionSpec as P

adapter_scale = 0.5
cores = 2
chunk_count = 4
split_chunks = 2
cross_chunks = 1
mesh_ids = pl.DeviceIdType.MESH


def dot(left, right, left_dim, right_dim):
    return lax.dot_general(
        left, right, (((left_dim,), (right_dim,)), ((), ())), preferred_element_type=jnp.float32
    )


def partner(position, offset, size):
    if size & (size - 1):
        return lax.rem(position + offset, size)
    bit = 1
    while bit < size:
        if offset & bit:
            position = position + bit - 2 * bit * lax.rem(position // bit, 2)
        bit *= 2
    return position


def lane_tile(piece_width):
    return 384 if piece_width % 384 == 0 else piece_width


def crossing_chunks(chunks, chips):
    return min(cross_chunks, chunks - 2) if chips % 2 == 0 else 0


def kernel(
    dp, fsdp,
    ids_ref, fill_ref, down_ref, up_ref, w_ref, x_hbm, dy_hbm,
    y_out, dx_out, down_out, up_out,
    x, dy, dy_slices, catalog, outgoing, arrived, returned, sums_in, frozen, id_rows,
    pick, put, u_rows, v_rows, u_cols, v_cols, up_blocks, total,
    load_sem, own_sem, s1_send, s1_recv, id_send, id_recv, p_send, p_recv, t_send, t_recv,
    g_send, g_recv, right_send, right_recv, left_send, left_recv, w2_send, w2_recv, relay_recv,
    x_send, x_recv, c_send, c_recv, crossed, w3_send, w3_recv,
):
    my_dp, me = lax.axis_index("dp"), lax.axis_index("fsdp")
    chunks, _, own, _, piece_width = catalog.shape
    per_dev, rank_rows, block_rows = u_rows.shape[1:]
    count_dev, model_width = x.shape
    width = dy.shape[1]
    features, outputs = model_width // fsdp, width // fsdp
    block_group = per_dev * rank_rows
    lanes = fsdp * block_group
    total_rows = dp * own * rank_rows
    chips = fsdp // cores
    chip, core = me // cores, lax.rem(me, cores)
    tile_lanes = lane_tile(piece_width)
    parts = piece_width // tile_lanes
    crossing = crossing_chunks(chunks, chips)
    direct = chunks - crossing
    half = fsdp // 2
    first = me // half * half
    local, across = me - first, lax.rem(me + half, fsdp)
    two_hops = dp == 4
    share_half = frozen.shape[2] // 2
    last = chunks - 1
    whole = max(chunks - split_chunks, 0)

    def peer(offset):
        return lax.rem(me + offset, fsdp)

    def column(slice_index):
        return pl.ds(pl.multiple_of(slice_index * features, features), features)

    loads = [
        pltpu.make_async_copy(x_hbm, x, load_sem.at[0]),
        pltpu.make_async_copy(dy_hbm, dy, load_sem.at[1]),
        pltpu.make_async_copy(w_ref, frozen.at[me], load_sem.at[2]),
    ]
    owns = []
    for k in range(chunks):
        ranks = pl.ds(k * rank_rows, rank_rows)
        place = catalog.at[k, my_dp]
        if outputs % 128 == 0:
            owns.append((
                pltpu.make_async_copy(
                    down_ref.at[:, ranks, :], place.at[:, :, pl.ds(0, features)], own_sem.at[0, k]
                ),
                pltpu.make_async_copy(
                    up_ref.at[:, ranks, :], place.at[:, :, pl.ds(features, outputs)], own_sem.at[1, k]
                ),
            ))
        else:
            owns.append((pltpu.make_async_copy(down_ref.at[:, ranks, :], place, own_sem.at[0, k]),))
    for copies in owns:
        for copy in copies:
            copy.start()

    lane_block = lax.shift_right_logical(
        lax.broadcasted_iota(jnp.int32, (8, lanes), 1), rank_rows.bit_length() - 1
    )
    mine = jnp.zeros((8, lanes), jnp.int32)
    for block in range(per_dev):
        mine = jnp.where(lane_block == me * per_dev + block, ids_ref[block] + 1, mine)
    id_rows[me] = mine

    barrier = pltpu.get_barrier_semaphore()

    @pl.loop(1, fsdp)
    def _(offset):
        pl.semaphore_signal(barrier, inc=1, device_id=(my_dp, peer(offset)), device_id_type=mesh_ids)

    for offset in range(1, dp):
        pl.semaphore_signal(
            barrier, inc=1, device_id=(partner(my_dp, offset, dp), me), device_id_type=mesh_ids
        )
    pl.semaphore_wait(barrier, fsdp + dp - 2)

    def remote(source, target, send, recv, device):
        return pltpu.make_async_remote_copy(
            src_ref=source, dst_ref=target, send_sem=send, recv_sem=recv,
            device_id=device, device_id_type=mesh_ids,
        )

    def wait_group(array, semaphore):
        pltpu.make_async_copy(array, array, semaphore).wait()

    others, dp_others = pl.ds(0, fsdp - 1), pl.ds(0, dp - 1)

    def id_group():
        return id_rows.at[others]

    def s1_group(k):
        return catalog.at[k, dp_others]

    def p_group(k):
        return arrived.at[k, others] if k < direct else arrived.at[k, pl.ds(0, fsdp - 2)]

    def t_group(k, part):
        return returned.at[k, others, :, lanes_of(k, part)]

    def g_group(k, part):
        return sums_in.at[k, dp_others, :, :, lanes_of(k, part)]

    def w2_group(shares=dp - 1):
        return frozen.at[0, pl.ds(0, shares)]

    def id_copy(offset):
        return remote(
            id_rows.at[me], id_rows.at[me], id_send, id_recv,
            (my_dp, peer(offset)),
        )

    def s1_copy(k, offset):
        return remote(
            catalog.at[k, my_dp], catalog.at[k, my_dp], s1_send.at[k], s1_recv.at[k],
            (partner(my_dp, offset, dp), me),
        )

    def p_copy(k, offset):
        return remote(
            outgoing.at[k, peer(offset)], arrived.at[k, me], p_send.at[k],
            p_recv.at[k], (my_dp, peer(offset)),
        )

    def lanes_of(k, part):
        return pl.ds(0, piece_width) if k < whole else pl.ds(part * tile_lanes, tile_lanes)

    def slot_of(k, part):
        return k if k < whole else whole + (k - whole) * parts + part

    def half_copies(k, offset):
        target = lax.rem(local + offset, half)
        return [
            remote(
                outgoing.at[k, slot * half + target], arrived.at[k, place], p_send.at[k], p_recv.at[k],
                (my_dp, first + target),
            )
            for slot, place in enumerate((me, across))
        ]

    def cross_copy(k):
        return remote(
            catalog.at[k, my_dp], crossed.at[k - direct, my_dp], x_send.at[k - direct],
            x_recv.at[k - direct], (my_dp, across),
        )

    def crossed_copy(k, offset):
        return remote(
            crossed.at[k - direct, my_dp], crossed.at[k - direct, my_dp], c_send.at[k - direct],
            c_recv.at[k - direct], (partner(my_dp, offset, dp), me),
        )

    def spread_crossed(k):
        cross_copy(k).wait_recv()
        for offset in range(1, dp):
            crossed_copy(k, offset).start()

    def t_copy(k, offset, part=0):
        sent = lanes_of(k, part)
        return remote(
            outgoing.at[k, peer(offset), :, sent], returned.at[k, me, :, sent],
            t_send.at[slot_of(k, part)], t_recv.at[slot_of(k, part)], (my_dp, peer(offset)),
        )

    def g_copy(k, offset, part=0):
        other = partner(my_dp, offset, dp)
        sent = lanes_of(k, part)
        return remote(
            catalog.at[k, other, :, :, sent], sums_in.at[k, my_dp, :, :, sent],
            g_send.at[slot_of(k, part)], g_recv.at[slot_of(k, part)], (other, me),
        )

    def parts_of(k):
        return range(parts) if k >= whole else range(1)

    def right_copy(step):
        source = w_ref.at[my_dp] if step == 0 else frozen.at[me - cores * step, my_dp]
        return remote(
            source, frozen.at[me - cores * step, my_dp], right_send.at[step], right_recv.at[step],
            (my_dp, me + cores),
        )

    def left_copy(step):
        source = w_ref.at[my_dp] if step == 0 else frozen.at[me + cores * step, my_dp]
        return remote(
            source, frozen.at[me + cores * step, my_dp], left_send.at[step], left_recv.at[step],
            (my_dp, me - cores),
        )

    def sends_right(step):
        return (chip >= step) & (chip + 1 < chips)

    def sends_left(step):
        return (chip + step < chips) & (chip >= 1)

    def gets_right(step):
        return chip >= step + 1

    def gets_left(step):
        return chip + step + 1 < chips

    def w2_copy(from_chip, offset):
        row = from_chip * cores + core
        return remote(
            frozen.at[row, my_dp], frozen.at[row, my_dp], w2_send.at[from_chip],
            w2_recv.at[from_chip], (partner(my_dp, offset, dp), me),
        )

    def w3_copy(from_chip):
        row = from_chip * cores + core
        return remote(
            frozen.at[row], frozen.at[row], w3_send.at[from_chip], w3_recv.at[from_chip],
            (my_dp, me + 1 - 2 * core),
        )

    def relay(step):
        @pl.when(gets_right(step))
        def _():
            right_copy(step).wait_recv()

        @pl.when(gets_left(step))
        def _():
            left_copy(step).wait_recv()

        if step + 1 < chips - 1:

            @pl.when(sends_right(step + 1))
            def _():
                right_copy(step + 1).start()

            @pl.when(sends_left(step + 1))
            def _():
                left_copy(step + 1).start()

    def relay_copy(from_chip, source, target, part):
        row = from_chip * cores + core
        rows = frozen.at[row, partner(my_dp, source, dp), pl.ds(part * share_half, share_half)]
        return remote(
            rows, rows, w2_send.at[from_chip], relay_recv.at[from_chip],
            (partner(my_dp, target, dp), me),
        )

    def each_arrived(step, action):
        @pl.when(gets_right(step))
        def _():
            action(chip - step - 1)

        @pl.when(gets_left(step))
        def _():
            action(chip + step + 1)

    def spread_shares(step):
        def send(from_chip):
            for offset in range(1, 3 if two_hops else dp):
                w2_copy(from_chip, offset).start()

        each_arrived(step, send)

    def relay_shares(step):
        def send(from_chip):
            wait_group(w2_group(2), w2_recv.at[from_chip])
            relay_copy(from_chip, 1, 2, 0).start()
            relay_copy(from_chip, 2, 1, 1).start()

        if two_hops:
            each_arrived(step, send)

    @pl.loop(1, fsdp)
    def _(offset):
        id_copy(offset).start()

    def share_catalog(k):
        for copy in owns[k]:
            copy.wait()
        for offset in range(1, dp):
            s1_copy(k, offset).start()

    share_catalog(0)

    @pl.when(sends_right(0))
    def _():
        right_copy(0).start()

    @pl.when(sends_left(0))
    def _():
        left_copy(0).start()

    for k in range(1, chunks):
        share_catalog(k)
    for copy in loads:
        copy.start()

    wait_group(id_group(), id_recv)

    numbers = id_rows[0]
    for position in range(1, fsdp):
        numbers = numbers + id_rows[position]
    numbers = numbers[0:1, :] - 1
    shift = rank_rows.bit_length() - 1
    row = lax.broadcasted_iota(jnp.int32, (total_rows, lanes), 0)
    lane = lax.broadcasted_iota(jnp.int32, (total_rows, lanes), 1)
    same_rank = (row & (rank_rows - 1)) == (lane & (rank_rows - 1))
    same_adapter = lax.shift_right_logical(row, shift) == numbers
    hot = jnp.where(same_rank & same_adapter, 1.0, 0.0)
    put[...] = hot.astype(jnp.bfloat16)
    pick[...] = hot.T.astype(jnp.bfloat16)

    def choose(k):
        wait_group(s1_group(k), s1_recv.at[k])
        tables, picked, targets = [catalog.at[k]], pick[...], fsdp
        if k >= direct:
            wait_group(s1_group(k), c_recv.at[k - direct])
            tables.append(crossed.at[k - direct])
            rows = pl.ds(pl.multiple_of(first * block_group, half * block_group), half * block_group)
            picked, targets = pick[rows, :], half
        for slot, table_ref in enumerate(tables):
            for start in range(0, piece_width, tile_lanes):
                tile = slice(start, start + tile_lanes)
                table = table_ref[:, :, :, tile].reshape(total_rows, tile_lanes)
                chosen = dot(picked, table, 1, 0).astype(jnp.bfloat16)
                outgoing[k, slot * half : slot * half + targets, :, tile] = chosen.reshape(
                    targets, block_group, tile_lanes
                )
        if k < direct:
            arrived[k, me] = outgoing[k, me]

            @pl.loop(1, fsdp)
            def _(offset):
                p_copy(k, offset).start()

        else:
            arrived[k, me] = outgoing[k, local]
            arrived[k, across] = outgoing[k, half + local]

            @pl.loop(1, half)
            def _(offset):
                for copy in half_copies(k, offset):
                    copy.start()

    def low_rank(k):
        wait_group(p_group(k), p_recv.at[k])

        zero = jnp.zeros((rank_rows, block_rows), jnp.float32)

        def gather_low(index, sums):
            result = []
            for block in range(per_dev):
                tokens = slice(block * block_rows, (block + 1) * block_rows)
                ranks = slice(block * rank_rows, (block + 1) * rank_rows)
                u = dot(arrived[k, index, ranks, :features], x[tokens, column(index)], 1, 1)
                v = dot(arrived[k, index, ranks, features:], dy_slices[index, tokens, :], 1, 1)
                result += [sums[2 * block] + u, sums[2 * block + 1] + v]
            return tuple(result)

        sums = lax.fori_loop(0, fsdp, gather_low, (zero,) * (2 * per_dev))
        token = lax.broadcasted_iota(jnp.int32, (rank_rows, block_rows), 1)
        for block in range(per_dev):
            live = (token < fill_ref[block]).astype(jnp.float32)
            u_rows[k, block] = (sums[2 * block] * live).astype(jnp.bfloat16)
            v_rows[k, block] = (sums[2 * block + 1] * live).astype(jnp.bfloat16)

        def terms_of(index):
            for block in range(per_dev):
                tokens = slice(block * block_rows, (block + 1) * block_rows)
                ranks = slice(block * rank_rows, (block + 1) * rank_rows)
                down = dot(v_rows[k, block], x[tokens, column(index)], 1, 0)
                up = dot(u_rows[k, block], dy_slices[index, tokens, :], 1, 0)
                outgoing[k, index, ranks, :features] = down.astype(jnp.bfloat16)
                outgoing[k, index, ranks, features:] = up.astype(jnp.bfloat16)

        wait_group(p_group(k), p_send.at[k])

        @pl.loop(1, fsdp)
        def _(offset):
            terms_of(peer(offset))
            if k < whole:

                @pl.when(offset > 1)
                def _():
                    t_copy(k, offset - 1).start()

        terms_of(me)
        if k < whole:
            t_copy(k, fsdp - 1).start()
        else:
            for part in parts_of(k):

                @pl.loop(1, fsdp)
                def _(offset):
                    t_copy(k, offset, part).start()

        returned[k, me] = outgoing[k, me]

    def combine(k, part=0):
        if part == 0:
            wait_group(s1_group(k), s1_send.at[k])
            if k >= direct:
                cross_copy(k).wait_send()

        wait_group(t_group(k, part), t_recv.at[slot_of(k, part)])

        starts = [part * tile_lanes] if k >= whole else range(0, piece_width, tile_lanes)
        for start in starts:
            tile = slice(start, start + tile_lanes)
            terms = returned[k, :, :, tile].reshape(lanes, tile_lanes)
            added = dot(put[...], terms, 1, 0).astype(jnp.bfloat16)
            catalog[k, :, :, :, tile] = added.reshape(dp, own, rank_rows, tile_lanes)
        for offset in range(1, dp):
            g_copy(k, offset, part).start()
        for start in starts:
            tile = slice(start, start + tile_lanes)
            sums_in[k, my_dp, :, :, tile] = catalog[k, my_dp, :, :, tile]

    def finish(k):
        for part in parts_of(k):
            wait_group(g_group(k, part), g_recv.at[slot_of(k, part)])
        added = sums_in[k, 0].astype(jnp.float32)
        for position in range(1, dp):
            added = added + sums_in[k, position].astype(jnp.float32)
        added = adapter_scale * added
        ranks = slice(k * rank_rows, (k + 1) * rank_rows)
        down_out[:, ranks, :] = added[:, :, :features]
        up_out[:, ranks, :] = added[:, :, features:]

    def columns_of_low():
        for block in range(per_dev):
            for rows, columns in ((u_rows, u_cols), (v_rows, v_cols)):
                whole = jnp.concatenate([rows[k, block] for k in range(chunks)], axis=0)
                columns[block] = whole.astype(jnp.float32).T.astype(jnp.bfloat16)
            for index in range(fsdp):
                part = slice(index * outputs, (index + 1) * outputs)
                ranks = slice(block * rank_rows, (block + 1) * rank_rows)
                for k in range(chunks):
                    up_blocks[block, k * rank_rows : (k + 1) * rank_rows, part] = arrived[
                        k, index, ranks, features:
                    ]

    def base_values(first, end):
        @pl.loop(first, end)
        def _(index):
            product = dot(x[:, column(index)], frozen[index].reshape(features, width), 1, 0)

            @pl.when(index == 0)
            def _():
                total[...] = product

            @pl.when(index > 0)
            def _():
                total[...] += product

    def base_grads(first, end):
        @pl.loop(first, end)
        def _(index):
            base_grad = dot(dy[...], frozen[index].reshape(features, width), 1, 1)
            for block in range(per_dev):
                tokens = slice(block * block_rows, (block + 1) * block_rows)
                ranks = slice(block * rank_rows, (block + 1) * rank_rows)
                down = jnp.concatenate(
                    [arrived[k, index, ranks, :features] for k in range(chunks)], axis=0
                )
                pulled = dot(v_cols[block], down, 1, 0).astype(jnp.bfloat16).astype(jnp.float32)
                mixed = base_grad[tokens, :] + adapter_scale * pulled
                dx_out[tokens, column(index)] = mixed.astype(jnp.bfloat16)

    def last_values():
        for block in range(per_dev):
            tokens = slice(block * block_rows, (block + 1) * block_rows)
            lifted = dot(u_cols[block], up_blocks[block], 1, 0)
            lifted = lifted.astype(jnp.bfloat16).astype(jnp.float32)
            y_out[tokens, :] = (total[tokens, :] + adapter_scale * lifted).astype(jnp.bfloat16)

    def pass_core(step):
        def give(from_chip):
            if two_hops:
                wait_group(w2_group(1), relay_recv.at[from_chip])
            else:
                wait_group(w2_group(), w2_recv.at[from_chip])
            w3_copy(from_chip).start()

        each_arrived(step, give)

    hops = chips - 1
    relay(0)
    for k in range(direct, chunks):
        cross_copy(k).start()
    choose(0)
    for copy in loads:
        copy.wait()
    w3_copy(chip).start()
    for index in range(fsdp):
        dy_slices[index] = dy[:, index * outputs : (index + 1) * outputs]
    choose(1)
    for k in range(direct, chunks):
        spread_crossed(k)
    spread_shares(0)
    for step in range(1, min(2, hops)):
        relay(step)
        spread_shares(step)
    low_rank(0)
    choose(2)
    low_rank(1)
    relay_shares(0)
    choose(3)
    for step in range(2, hops):
        relay(step)
        spread_shares(step)
    relay_shares(1)
    combine(0)
    for step in range(2, hops):
        relay_shares(step)
    low_rank(2)
    for step in range(hops):
        pass_core(step)
    low_rank(3)
    combine(1)
    columns_of_low()
    for from_chip in range(chips):
        w3_copy(from_chip).wait_recv()

    order = [(k, part) for k in (last - 1, last) for part in parts_of(k)]
    middle, quarter = fsdp // 2, fsdp // 4
    fill = [(base_values, 0, middle), (base_values, middle, fsdp), (base_grads, 0, quarter)]
    fill += [(base_grads, quarter, middle)]
    for k, part in order:
        if fill:
            work, start, end = fill.pop(0)
            work(start, end)
        combine(k, part)
    for work, start, end in fill + [(base_grads, middle, fsdp)]:
        work(start, end)
    last_values()
    for k in range(chunks):
        finish(k)

    def drain():
        for k in range(direct, chunks):
            wait_group(s1_group(k), c_send.at[k - direct])
        wait_group(id_group(), id_send)
        for k in range(chunks):
            for part in parts_of(k):
                slot = slot_of(k, part)
                wait_group(t_group(k, part), t_send.at[slot])
                wait_group(g_group(k, part), g_send.at[slot])
        for step in range(hops):

            @pl.when(sends_right(step))
            def _():
                right_copy(step).wait_send()

            @pl.when(sends_left(step))
            def _():
                left_copy(step).wait_send()

        for from_chip in range(chips):

            @pl.when(from_chip != chip)
            def _():
                wait_group(w2_group(), w2_send.at[from_chip])

            w3_copy(from_chip).wait_send()

    drain()


def store_kernel(y, dx, down, up, y_out, dx_out, down_out, up_out, semaphores):
    pieces = 4
    rows = dx.shape[0] // pieces
    copies = []
    for piece in range(pieces):
        part = pl.ds(piece * rows, rows)
        copies.append(pltpu.make_async_copy(dx.at[part], dx_out.at[part], semaphores.at[piece]))
    for index, (source, target) in enumerate(((down, down_out), (y, y_out), (up, up_out))):
        copies.append(pltpu.make_async_copy(source, target, semaphores.at[pieces + index]))
    for copy in copies:
        copy.start()
    for copy in copies:
        copy.wait()


def store(results):
    vmem, anywhere = pl.BlockSpec(memory_space=pltpu.VMEM), pl.BlockSpec(memory_space=pl.ANY)
    return pl.pallas_call(
        store_kernel,
        out_shape=tuple(jax.ShapeDtypeStruct(array.shape, array.dtype) for array in results),
        in_specs=[vmem] * len(results),
        out_specs=(anywhere,) * len(results),
        scratch_shapes=[pltpu.SemaphoreType.DMA((7,))],
        compiler_params=pltpu.CompilerParams(vmem_limit_bytes=16_000_000),
        name="store",
    )(*results)


def body(
    tokens,
    frozen_value_weight,
    adapter_down_weight,
    adapter_up_weight,
    output_gradient,
    adapter_per_block,
    block_live_count,
):
    dp, fsdp = lax.axis_size("dp"), lax.axis_size("fsdp")
    count_dev, model_width = tokens.shape
    width = output_gradient.shape[1]
    per_dev = adapter_per_block.shape[0]
    block_rows = count_dev // per_dev
    own, features, rank = adapter_down_weight.shape
    outputs = adapter_up_weight.shape[2]
    piece_width = features + outputs
    chunks, rows_chunk = chunk_count, rank // chunk_count
    split = min(split_chunks, chunks)
    steps = chunks - split + split * (piece_width // lane_tile(piece_width))
    chips = fsdp // cores
    share_rows = frozen_value_weight.shape[0] // dp
    crossing = crossing_chunks(chunks, chips)
    down, up = adapter_down_weight.transpose(0, 2, 1), adapter_up_weight
    if outputs % 128:
        down = jnp.concatenate([down, up], axis=2)
    weight = frozen_value_weight.reshape(dp, share_rows, width)
    block_group = per_dev * rows_chunk
    lanes = fsdp * block_group
    total_rows = dp * own * rows_chunk
    bf16, f32 = jnp.bfloat16, jnp.float32
    anywhere = pl.BlockSpec(memory_space=pl.ANY)
    scalars = pl.BlockSpec(memory_space=pltpu.SMEM)
    dma = pltpu.SemaphoreType.DMA
    scratch = [
        pltpu.VMEM((count_dev, model_width), bf16),
        pltpu.VMEM((count_dev, width), bf16),
        pltpu.VMEM((fsdp, count_dev, outputs), bf16),
        pltpu.VMEM((chunks, dp, own, rows_chunk, piece_width), bf16),
        pltpu.VMEM((chunks, fsdp, block_group, piece_width), bf16),
        pltpu.VMEM((chunks, fsdp, block_group, piece_width), bf16),
        pltpu.VMEM((chunks, fsdp, block_group, piece_width), bf16),
        pltpu.VMEM((chunks, dp, own, rows_chunk, piece_width), bf16),
        pltpu.VMEM((fsdp, dp, share_rows, width), bf16),
        pltpu.VMEM((fsdp, 8, lanes), jnp.int32),
        pltpu.VMEM((lanes, total_rows), bf16),
        pltpu.VMEM((total_rows, lanes), bf16),
        pltpu.VMEM((chunks, per_dev, rows_chunk, block_rows), bf16),
        pltpu.VMEM((chunks, per_dev, rows_chunk, block_rows), bf16),
        pltpu.VMEM((per_dev, block_rows, rank), bf16),
        pltpu.VMEM((per_dev, block_rows, rank), bf16),
        pltpu.VMEM((per_dev, rank, width), bf16),
        pltpu.VMEM((count_dev, width), f32),
        dma((3,)),
        dma((2, chunks)),
        dma((chunks,)), dma((chunks,)),
        dma, dma,
        dma((chunks,)), dma((chunks,)),
        dma((steps,)), dma((steps,)),
        dma((steps,)), dma((steps,)),
        dma((chips - 1,)), dma((chips - 1,)),
        dma((chips - 1,)), dma((chips - 1,)),
        dma((chips,)), dma((chips,)), dma((chips,)),
        dma((max(crossing, 1),)), dma((max(crossing, 1),)),
        dma((max(crossing, 1),)), dma((max(crossing, 1),)),
        pltpu.VMEM((max(crossing, 1), dp, own, rows_chunk, piece_width), bf16),
        dma((chips,)), dma((chips,)),
    ]
    results = pl.pallas_call(
        functools.partial(kernel, dp, fsdp),
        out_shape=(
            pltpu.VMEM((count_dev, width), bf16),
            pltpu.VMEM((count_dev, model_width), bf16),
            pltpu.VMEM((own, rank, features), f32),
            pltpu.VMEM((own, rank, outputs), f32),
        ),
        in_specs=[scalars, scalars] + [anywhere] * 5,
        out_specs=(pl.BlockSpec(memory_space=pltpu.VMEM),) * 4,
        scratch_shapes=scratch,
        compiler_params=pltpu.CompilerParams(
            collective_id=0, has_side_effects=True, vmem_limit_bytes=56_500_000
        ),
        name="lora",
    )(adapter_per_block, block_live_count, down, up, weight, tokens, output_gradient)
    values, input_gradient, grad_down, grad_up = store(results)
    return values, input_gradient, grad_down.transpose(0, 2, 1), grad_up


def solution(mesh):
    placed = (
        P(("dp", "fsdp"), None),
        P("fsdp", None),
        P("dp", "fsdp", None),
        P("dp", None, "fsdp"),
        P(("dp", "fsdp"), None),
        P(("dp", "fsdp")),
        P(("dp", "fsdp")),
    )
    return jax.shard_map(
        body,
        mesh=mesh,
        in_specs=placed,
        out_specs=(
            P(("dp", "fsdp"), None),
            P(("dp", "fsdp"), None),
            P("dp", "fsdp", None),
            P("dp", None, "fsdp"),
        ),
        check_vma=False,
    )
```

```python
import functools

import jax
import jax.numpy as jnp
from jax import lax
from jax.experimental import pallas as pl
from jax.experimental.pallas import tpu as pltpu
from jax.sharding import PartitionSpec as P

adapter_scale = 0.5
cores = 2
chunk_count = 4
split_chunks = 2
cross_chunks = 1
mesh_ids = pl.DeviceIdType.MESH


def dot(left, right, left_dim, right_dim):
    return lax.dot_general(
        left, right, (((left_dim,), (right_dim,)), ((), ())), preferred_element_type=jnp.float32
    )


def partner(position, offset, size):
    if size & (size - 1):
        return lax.rem(position + offset, size)
    bit = 1
    while bit < size:
        if offset & bit:
            position = position + bit - 2 * bit * lax.rem(position // bit, 2)
        bit *= 2
    return position


def lane_tile(piece_width):
    return 384 if piece_width % 384 == 0 else piece_width


def crossing_chunks(chunks, chips):
    return min(cross_chunks, chunks - 2) if chips % 2 == 0 else 0


def kernel(
    dp, fsdp,
    ids_ref, fill_ref, down_ref, up_ref, w_ref, x_hbm, dy_hbm,
    y_out, dx_out, down_out, up_out,
    x, dy, dy_slices, catalog, outgoing, arrived, returned, sums_in, frozen, id_rows,
    pick, put, u_rows, v_rows, u_cols, v_cols, up_blocks, total,
    load_sem, own_sem, s1_send, s1_recv, id_send, id_recv, p_send, p_recv, t_send, t_recv,
    g_send, g_recv, right_send, right_recv, left_send, left_recv, w2_send, w2_recv, relay_recv,
    x_send, x_recv, c_send, c_recv, crossed, w3_send, w3_recv,
):
    my_dp, me = lax.axis_index("dp"), lax.axis_index("fsdp")
    chunks, _, own, _, piece_width = catalog.shape
    per_dev, rank_rows, block_rows = u_rows.shape[1:]
    count_dev, model_width = x.shape
    width = dy.shape[1]
    features, outputs = model_width // fsdp, width // fsdp
    block_group = per_dev * rank_rows
    lanes = fsdp * block_group
    total_rows = dp * own * rank_rows
    chips = fsdp // cores
    chip, core = me // cores, lax.rem(me, cores)
    tile_lanes = lane_tile(piece_width)
    parts = piece_width // tile_lanes
    crossing = crossing_chunks(chunks, chips)
    direct = chunks - crossing
    half = fsdp // 2
    first = me // half * half
    local, across = me - first, lax.rem(me + half, fsdp)
    two_hops = dp == 4
    share_half = frozen.shape[2] // 2
    last = chunks - 1
    whole = max(chunks - split_chunks, 0)

    def peer(offset):
        return lax.rem(me + offset, fsdp)

    def column(slice_index):
        return pl.ds(pl.multiple_of(slice_index * features, features), features)

    loads = [
        pltpu.make_async_copy(x_hbm, x, load_sem.at[0]),
        pltpu.make_async_copy(dy_hbm, dy, load_sem.at[1]),
        pltpu.make_async_copy(w_ref, frozen.at[me], load_sem.at[2]),
    ]
    owns = []
    for k in range(chunks):
        ranks = pl.ds(k * rank_rows, rank_rows)
        place = catalog.at[k, my_dp]
        if outputs % 128 == 0:
            owns.append((
                pltpu.make_async_copy(
                    down_ref.at[:, ranks, :], place.at[:, :, pl.ds(0, features)], own_sem.at[0, k]
                ),
                pltpu.make_async_copy(
                    up_ref.at[:, ranks, :], place.at[:, :, pl.ds(features, outputs)], own_sem.at[1, k]
                ),
            ))
        else:
            owns.append((pltpu.make_async_copy(down_ref.at[:, ranks, :], place, own_sem.at[0, k]),))
    for copies in owns:
        for copy in copies:
            copy.start()

    lane_block = lax.shift_right_logical(
        lax.broadcasted_iota(jnp.int32, (8, lanes), 1), rank_rows.bit_length() - 1
    )
    mine = jnp.zeros((8, lanes), jnp.int32)
    for block in range(per_dev):
        mine = jnp.where(lane_block == me * per_dev + block, ids_ref[block] + 1, mine)
    id_rows[me] = mine

    barrier = pltpu.get_barrier_semaphore()

    @pl.loop(1, fsdp)
    def _(offset):
        pl.semaphore_signal(barrier, inc=1, device_id=(my_dp, peer(offset)), device_id_type=mesh_ids)

    for offset in range(1, dp):
        pl.semaphore_signal(
            barrier, inc=1, device_id=(partner(my_dp, offset, dp), me), device_id_type=mesh_ids
        )
    pl.semaphore_wait(barrier, fsdp + dp - 2)

    def remote(source, target, send, recv, device):
        return pltpu.make_async_remote_copy(
            src_ref=source, dst_ref=target, send_sem=send, recv_sem=recv,
            device_id=device, device_id_type=mesh_ids,
        )

    def wait_group(array, semaphore):
        pltpu.make_async_copy(array, array, semaphore).wait()

    others, dp_others = pl.ds(0, fsdp - 1), pl.ds(0, dp - 1)

    def id_group():
        return id_rows.at[others]

    def s1_group(k):
        return catalog.at[k, dp_others]

    def p_group(k):
        return arrived.at[k, others] if k < direct else arrived.at[k, pl.ds(0, fsdp - 2)]

    def t_group(k, part):
        return returned.at[k, others, :, lanes_of(k, part)]

    def g_group(k, part):
        return sums_in.at[k, dp_others, :, :, lanes_of(k, part)]

    def w2_group(shares=dp - 1):
        return frozen.at[0, pl.ds(0, shares)]

    def id_copy(offset):
        return remote(
            id_rows.at[me], id_rows.at[me], id_send, id_recv,
            (my_dp, peer(offset)),
        )

    def s1_copy(k, offset):
        return remote(
            catalog.at[k, my_dp], catalog.at[k, my_dp], s1_send.at[k], s1_recv.at[k],
            (partner(my_dp, offset, dp), me),
        )

    def p_copy(k, offset):
        return remote(
            outgoing.at[k, peer(offset)], arrived.at[k, me], p_send.at[k],
            p_recv.at[k], (my_dp, peer(offset)),
        )

    def lanes_of(k, part):
        return pl.ds(0, piece_width) if k < whole else pl.ds(part * tile_lanes, tile_lanes)

    def slot_of(k, part):
        return k if k < whole else whole + (k - whole) * parts + part

    def half_copies(k, offset):
        target = lax.rem(local + offset, half)
        return [
            remote(
                outgoing.at[k, slot * half + target], arrived.at[k, place], p_send.at[k], p_recv.at[k],
                (my_dp, first + target),
            )
            for slot, place in enumerate((me, across))
        ]

    def cross_copy(k):
        return remote(
            catalog.at[k, my_dp], crossed.at[k - direct, my_dp], x_send.at[k - direct],
            x_recv.at[k - direct], (my_dp, across),
        )

    def crossed_copy(k, offset):
        return remote(
            crossed.at[k - direct, my_dp], crossed.at[k - direct, my_dp], c_send.at[k - direct],
            c_recv.at[k - direct], (partner(my_dp, offset, dp), me),
        )

    def spread_crossed(k):
        cross_copy(k).wait_recv()
        for offset in range(1, dp):
            crossed_copy(k, offset).start()

    def t_copy(k, offset, part=0):
        sent = lanes_of(k, part)
        return remote(
            outgoing.at[k, peer(offset), :, sent], returned.at[k, me, :, sent],
            t_send.at[slot_of(k, part)], t_recv.at[slot_of(k, part)], (my_dp, peer(offset)),
        )

    def g_copy(k, offset, part=0):
        other = partner(my_dp, offset, dp)
        sent = lanes_of(k, part)
        return remote(
            catalog.at[k, other, :, :, sent], sums_in.at[k, my_dp, :, :, sent],
            g_send.at[slot_of(k, part)], g_recv.at[slot_of(k, part)], (other, me),
        )

    def parts_of(k):
        return range(parts) if k >= whole else range(1)

    def right_copy(step):
        source = w_ref.at[my_dp] if step == 0 else frozen.at[me - cores * step, my_dp]
        return remote(
            source, frozen.at[me - cores * step, my_dp], right_send.at[step], right_recv.at[step],
            (my_dp, me + cores),
        )

    def left_copy(step):
        source = w_ref.at[my_dp] if step == 0 else frozen.at[me + cores * step, my_dp]
        return remote(
            source, frozen.at[me + cores * step, my_dp], left_send.at[step], left_recv.at[step],
            (my_dp, me - cores),
        )

    def sends_right(step):
        return (chip >= step) & (chip + 1 < chips)

    def sends_left(step):
        return (chip + step < chips) & (chip >= 1)

    def gets_right(step):
        return chip >= step + 1

    def gets_left(step):
        return chip + step + 1 < chips

    def w2_copy(from_chip, offset):
        row = from_chip * cores + core
        return remote(
            frozen.at[row, my_dp], frozen.at[row, my_dp], w2_send.at[from_chip],
            w2_recv.at[from_chip], (partner(my_dp, offset, dp), me),
        )

    def w3_copy(from_chip):
        row = from_chip * cores + core
        return remote(
            frozen.at[row], frozen.at[row], w3_send.at[from_chip], w3_recv.at[from_chip],
            (my_dp, me + 1 - 2 * core),
        )

    def relay(step):
        @pl.when(gets_right(step))
        def _():
            right_copy(step).wait_recv()

        @pl.when(gets_left(step))
        def _():
            left_copy(step).wait_recv()

        if step + 1 < chips - 1:

            @pl.when(sends_right(step + 1))
            def _():
                right_copy(step + 1).start()

            @pl.when(sends_left(step + 1))
            def _():
                left_copy(step + 1).start()

    def relay_copy(from_chip, source, target, part):
        row = from_chip * cores + core
        rows = frozen.at[row, partner(my_dp, source, dp), pl.ds(part * share_half, share_half)]
        return remote(
            rows, rows, w2_send.at[from_chip], relay_recv.at[from_chip],
            (partner(my_dp, target, dp), me),
        )

    def each_arrived(step, action):
        @pl.when(gets_right(step))
        def _():
            action(chip - step - 1)

        @pl.when(gets_left(step))
        def _():
            action(chip + step + 1)

    def spread_shares(step):
        def send(from_chip):
            for offset in range(1, 3 if two_hops else dp):
                w2_copy(from_chip, offset).start()

        each_arrived(step, send)

    def relay_shares(step):
        def send(from_chip):
            wait_group(w2_group(2), w2_recv.at[from_chip])
            relay_copy(from_chip, 1, 2, 0).start()
            relay_copy(from_chip, 2, 1, 1).start()

        if two_hops:
            each_arrived(step, send)

    @pl.loop(1, fsdp)
    def _(offset):
        id_copy(offset).start()

    def share_catalog(k):
        for copy in owns[k]:
            copy.wait()
        for offset in range(1, dp):
            s1_copy(k, offset).start()

    share_catalog(0)

    @pl.when(sends_right(0))
    def _():
        right_copy(0).start()

    @pl.when(sends_left(0))
    def _():
        left_copy(0).start()

    for k in range(1, chunks):
        share_catalog(k)
    for copy in loads:
        copy.start()

    wait_group(id_group(), id_recv)

    numbers = id_rows[0]
    for position in range(1, fsdp):
        numbers = numbers + id_rows[position]
    numbers = numbers[0:1, :] - 1
    shift = rank_rows.bit_length() - 1
    row = lax.broadcasted_iota(jnp.int32, (total_rows, lanes), 0)
    lane = lax.broadcasted_iota(jnp.int32, (total_rows, lanes), 1)
    same_rank = (row & (rank_rows - 1)) == (lane & (rank_rows - 1))
    same_adapter = lax.shift_right_logical(row, shift) == numbers
    hot = jnp.where(same_rank & same_adapter, 1.0, 0.0)
    put[...] = hot.astype(jnp.bfloat16)
    pick[...] = hot.T.astype(jnp.bfloat16)

    def choose(k):
        wait_group(s1_group(k), s1_recv.at[k])
        tables, picked, targets = [catalog.at[k]], pick[...], fsdp
        if k >= direct:
            wait_group(s1_group(k), c_recv.at[k - direct])
            tables.append(crossed.at[k - direct])
            rows = pl.ds(pl.multiple_of(first * block_group, half * block_group), half * block_group)
            picked, targets = pick[rows, :], half
        for slot, table_ref in enumerate(tables):
            for start in range(0, piece_width, tile_lanes):
                tile = slice(start, start + tile_lanes)
                table = table_ref[:, :, :, tile].reshape(total_rows, tile_lanes)
                chosen = dot(picked, table, 1, 0).astype(jnp.bfloat16)
                outgoing[k, slot * half : slot * half + targets, :, tile] = chosen.reshape(
                    targets, block_group, tile_lanes
                )
        if k < direct:
            arrived[k, me] = outgoing[k, me]

            @pl.loop(1, fsdp)
            def _(offset):
                p_copy(k, offset).start()

        else:
            arrived[k, me] = outgoing[k, local]
            arrived[k, across] = outgoing[k, half + local]

            @pl.loop(1, half)
            def _(offset):
                for copy in half_copies(k, offset):
                    copy.start()

    def low_rank(k):
        wait_group(p_group(k), p_recv.at[k])

        zero = jnp.zeros((rank_rows, block_rows), jnp.float32)

        def gather_low(index, sums):
            result = []
            for block in range(per_dev):
                tokens = slice(block * block_rows, (block + 1) * block_rows)
                ranks = slice(block * rank_rows, (block + 1) * rank_rows)
                u = dot(arrived[k, index, ranks, :features], x[tokens, column(index)], 1, 1)
                v = dot(arrived[k, index, ranks, features:], dy_slices[index, tokens, :], 1, 1)
                result += [sums[2 * block] + u, sums[2 * block + 1] + v]
            return tuple(result)

        sums = lax.fori_loop(0, fsdp, gather_low, (zero,) * (2 * per_dev))
        token = lax.broadcasted_iota(jnp.int32, (rank_rows, block_rows), 1)
        for block in range(per_dev):
            live = (token < fill_ref[block]).astype(jnp.float32)
            u_rows[k, block] = (sums[2 * block] * live).astype(jnp.bfloat16)
            v_rows[k, block] = (sums[2 * block + 1] * live).astype(jnp.bfloat16)

        def terms_of(index):
            for block in range(per_dev):
                tokens = slice(block * block_rows, (block + 1) * block_rows)
                ranks = slice(block * rank_rows, (block + 1) * rank_rows)
                down = dot(v_rows[k, block], x[tokens, column(index)], 1, 0)
                up = dot(u_rows[k, block], dy_slices[index, tokens, :], 1, 0)
                outgoing[k, index, ranks, :features] = down.astype(jnp.bfloat16)
                outgoing[k, index, ranks, features:] = up.astype(jnp.bfloat16)

        wait_group(p_group(k), p_send.at[k])

        @pl.loop(1, fsdp)
        def _(offset):
            terms_of(peer(offset))
            if k < whole:

                @pl.when(offset > 1)
                def _():
                    t_copy(k, offset - 1).start()

        terms_of(me)
        if k < whole:
            t_copy(k, fsdp - 1).start()
        else:
            for part in parts_of(k):

                @pl.loop(1, fsdp)
                def _(offset):
                    t_copy(k, offset, part).start()

        returned[k, me] = outgoing[k, me]

    def combine(k, part=0):
        if part == 0:
            wait_group(s1_group(k), s1_send.at[k])
            if k >= direct:
                cross_copy(k).wait_send()

        wait_group(t_group(k, part), t_recv.at[slot_of(k, part)])

        starts = [part * tile_lanes] if k >= whole else range(0, piece_width, tile_lanes)
        for start in starts:
            tile = slice(start, start + tile_lanes)
            terms = returned[k, :, :, tile].reshape(lanes, tile_lanes)
            added = dot(put[...], terms, 1, 0).astype(jnp.bfloat16)
            catalog[k, :, :, :, tile] = added.reshape(dp, own, rank_rows, tile_lanes)
        for offset in range(1, dp):
            g_copy(k, offset, part).start()
        for start in starts:
            tile = slice(start, start + tile_lanes)
            sums_in[k, my_dp, :, :, tile] = catalog[k, my_dp, :, :, tile]

    def finish(k):
        for part in parts_of(k):
            wait_group(g_group(k, part), g_recv.at[slot_of(k, part)])
        added = sums_in[k, 0].astype(jnp.float32)
        for position in range(1, dp):
            added = added + sums_in[k, position].astype(jnp.float32)
        added = adapter_scale * added
        ranks = slice(k * rank_rows, (k + 1) * rank_rows)
        down_out[:, ranks, :] = added[:, :, :features]
        up_out[:, ranks, :] = added[:, :, features:]

    def columns_of_low():
        for block in range(per_dev):
            for rows, columns in ((u_rows, u_cols), (v_rows, v_cols)):
                whole = jnp.concatenate([rows[k, block] for k in range(chunks)], axis=0)
                columns[block] = whole.astype(jnp.float32).T.astype(jnp.bfloat16)
            for index in range(fsdp):
                part = slice(index * outputs, (index + 1) * outputs)
                ranks = slice(block * rank_rows, (block + 1) * rank_rows)
                for k in range(chunks):
                    up_blocks[block, k * rank_rows : (k + 1) * rank_rows, part] = arrived[
                        k, index, ranks, features:
                    ]

    def base_values(first, end):
        @pl.loop(first, end)
        def _(index):
            product = dot(x[:, column(index)], frozen[index].reshape(features, width), 1, 0)

            @pl.when(index == 0)
            def _():
                total[...] = product

            @pl.when(index > 0)
            def _():
                total[...] += product

    def base_grads(first, end):
        @pl.loop(first, end)
        def _(index):
            base_grad = dot(dy[...], frozen[index].reshape(features, width), 1, 1)
            for block in range(per_dev):
                tokens = slice(block * block_rows, (block + 1) * block_rows)
                ranks = slice(block * rank_rows, (block + 1) * rank_rows)
                down = jnp.concatenate(
                    [arrived[k, index, ranks, :features] for k in range(chunks)], axis=0
                )
                pulled = dot(v_cols[block], down, 1, 0).astype(jnp.bfloat16).astype(jnp.float32)
                mixed = base_grad[tokens, :] + adapter_scale * pulled
                dx_out[tokens, column(index)] = mixed.astype(jnp.bfloat16)

    def last_values():
        for block in range(per_dev):
            tokens = slice(block * block_rows, (block + 1) * block_rows)
            lifted = dot(u_cols[block], up_blocks[block], 1, 0)
            lifted = lifted.astype(jnp.bfloat16).astype(jnp.float32)
            y_out[tokens, :] = (total[tokens, :] + adapter_scale * lifted).astype(jnp.bfloat16)

    def pass_core(step):
        def give(from_chip):
            if two_hops:
                wait_group(w2_group(1), relay_recv.at[from_chip])
            else:
                wait_group(w2_group(), w2_recv.at[from_chip])
            w3_copy(from_chip).start()

        each_arrived(step, give)

    hops = chips - 1
    relay(0)
    for k in range(direct, chunks):
        cross_copy(k).start()
    choose(0)
    for copy in loads:
        copy.wait()
    w3_copy(chip).start()
    for index in range(fsdp):
        dy_slices[index] = dy[:, index * outputs : (index + 1) * outputs]
    choose(1)
    for k in range(direct, chunks):
        spread_crossed(k)
    spread_shares(0)
    for step in range(1, min(2, hops)):
        relay(step)
        spread_shares(step)
    low_rank(0)
    choose(2)
    low_rank(1)
    choose(3)
    relay_shares(0)
    for step in range(2, hops):
        relay(step)
        spread_shares(step)
    relay_shares(1)
    combine(0)
    for step in range(2, hops):
        relay_shares(step)
    low_rank(2)
    for step in range(hops):
        pass_core(step)
    low_rank(3)
    combine(1)
    columns_of_low()
    for from_chip in range(chips):
        w3_copy(from_chip).wait_recv()

    order = [(k, part) for k in (last - 1, last) for part in parts_of(k)]
    middle, quarter = fsdp // 2, fsdp // 4
    fill = [(base_values, 0, middle), (base_values, middle, fsdp), (base_grads, 0, quarter)]
    fill += [(base_grads, quarter, middle)]
    for k, part in order:
        if fill:
            work, start, end = fill.pop(0)
            work(start, end)
        combine(k, part)
    for work, start, end in fill + [(base_grads, middle, fsdp)]:
        work(start, end)
    last_values()
    for k in range(chunks):
        finish(k)

    def drain():
        for k in range(direct, chunks):
            wait_group(s1_group(k), c_send.at[k - direct])
        wait_group(id_group(), id_send)
        for k in range(chunks):
            for part in parts_of(k):
                slot = slot_of(k, part)
                wait_group(t_group(k, part), t_send.at[slot])
                wait_group(g_group(k, part), g_send.at[slot])
        for step in range(hops):

            @pl.when(sends_right(step))
            def _():
                right_copy(step).wait_send()

            @pl.when(sends_left(step))
            def _():
                left_copy(step).wait_send()

        for from_chip in range(chips):

            @pl.when(from_chip != chip)
            def _():
                wait_group(w2_group(), w2_send.at[from_chip])

            w3_copy(from_chip).wait_send()

    drain()


def store_kernel(y, dx, down, up, y_out, dx_out, down_out, up_out, semaphores):
    pieces = 4
    rows = dx.shape[0] // pieces
    copies = []
    for piece in range(pieces):
        part = pl.ds(piece * rows, rows)
        copies.append(pltpu.make_async_copy(dx.at[part], dx_out.at[part], semaphores.at[piece]))
    for index, (source, target) in enumerate(((down, down_out), (y, y_out), (up, up_out))):
        copies.append(pltpu.make_async_copy(source, target, semaphores.at[pieces + index]))
    for copy in copies:
        copy.start()
    for copy in copies:
        copy.wait()


def store(results):
    vmem, anywhere = pl.BlockSpec(memory_space=pltpu.VMEM), pl.BlockSpec(memory_space=pl.ANY)
    return pl.pallas_call(
        store_kernel,
        out_shape=tuple(jax.ShapeDtypeStruct(array.shape, array.dtype) for array in results),
        in_specs=[vmem] * len(results),
        out_specs=(anywhere,) * len(results),
        scratch_shapes=[pltpu.SemaphoreType.DMA((7,))],
        compiler_params=pltpu.CompilerParams(vmem_limit_bytes=16_000_000),
        name="store",
    )(*results)


def body(
    tokens,
    frozen_value_weight,
    adapter_down_weight,
    adapter_up_weight,
    output_gradient,
    adapter_per_block,
    block_live_count,
):
    dp, fsdp = lax.axis_size("dp"), lax.axis_size("fsdp")
    count_dev, model_width = tokens.shape
    width = output_gradient.shape[1]
    per_dev = adapter_per_block.shape[0]
    block_rows = count_dev // per_dev
    own, features, rank = adapter_down_weight.shape
    outputs = adapter_up_weight.shape[2]
    piece_width = features + outputs
    chunks, rows_chunk = chunk_count, rank // chunk_count
    split = min(split_chunks, chunks)
    steps = chunks - split + split * (piece_width // lane_tile(piece_width))
    chips = fsdp // cores
    share_rows = frozen_value_weight.shape[0] // dp
    crossing = crossing_chunks(chunks, chips)
    down, up = adapter_down_weight.transpose(0, 2, 1), adapter_up_weight
    if outputs % 128:
        down = jnp.concatenate([down, up], axis=2)
    weight = frozen_value_weight.reshape(dp, share_rows, width)
    block_group = per_dev * rows_chunk
    lanes = fsdp * block_group
    total_rows = dp * own * rows_chunk
    bf16, f32 = jnp.bfloat16, jnp.float32
    anywhere = pl.BlockSpec(memory_space=pl.ANY)
    scalars = pl.BlockSpec(memory_space=pltpu.SMEM)
    dma = pltpu.SemaphoreType.DMA
    scratch = [
        pltpu.VMEM((count_dev, model_width), bf16),
        pltpu.VMEM((count_dev, width), bf16),
        pltpu.VMEM((fsdp, count_dev, outputs), bf16),
        pltpu.VMEM((chunks, dp, own, rows_chunk, piece_width), bf16),
        pltpu.VMEM((chunks, fsdp, block_group, piece_width), bf16),
        pltpu.VMEM((chunks, fsdp, block_group, piece_width), bf16),
        pltpu.VMEM((chunks, fsdp, block_group, piece_width), bf16),
        pltpu.VMEM((chunks, dp, own, rows_chunk, piece_width), bf16),
        pltpu.VMEM((fsdp, dp, share_rows, width), bf16),
        pltpu.VMEM((fsdp, 8, lanes), jnp.int32),
        pltpu.VMEM((lanes, total_rows), bf16),
        pltpu.VMEM((total_rows, lanes), bf16),
        pltpu.VMEM((chunks, per_dev, rows_chunk, block_rows), bf16),
        pltpu.VMEM((chunks, per_dev, rows_chunk, block_rows), bf16),
        pltpu.VMEM((per_dev, block_rows, rank), bf16),
        pltpu.VMEM((per_dev, block_rows, rank), bf16),
        pltpu.VMEM((per_dev, rank, width), bf16),
        pltpu.VMEM((count_dev, width), f32),
        dma((3,)),
        dma((2, chunks)),
        dma((chunks,)), dma((chunks,)),
        dma, dma,
        dma((chunks,)), dma((chunks,)),
        dma((steps,)), dma((steps,)),
        dma((steps,)), dma((steps,)),
        dma((chips - 1,)), dma((chips - 1,)),
        dma((chips - 1,)), dma((chips - 1,)),
        dma((chips,)), dma((chips,)), dma((chips,)),
        dma((max(crossing, 1),)), dma((max(crossing, 1),)),
        dma((max(crossing, 1),)), dma((max(crossing, 1),)),
        pltpu.VMEM((max(crossing, 1), dp, own, rows_chunk, piece_width), bf16),
        dma((chips,)), dma((chips,)),
    ]
    results = pl.pallas_call(
        functools.partial(kernel, dp, fsdp),
        out_shape=(
            pltpu.VMEM((count_dev, width), bf16),
            pltpu.VMEM((count_dev, model_width), bf16),
            pltpu.VMEM((own, rank, features), f32),
            pltpu.VMEM((own, rank, outputs), f32),
        ),
        in_specs=[scalars, scalars] + [anywhere] * 5,
        out_specs=(pl.BlockSpec(memory_space=pltpu.VMEM),) * 4,
        scratch_shapes=scratch,
        compiler_params=pltpu.CompilerParams(
            collective_id=0, has_side_effects=True, vmem_limit_bytes=56_500_000
        ),
        name="lora",
    )(adapter_per_block, block_live_count, down, up, weight, tokens, output_gradient)
    values, input_gradient, grad_down, grad_up = store(results)
    return values, input_gradient, grad_down.transpose(0, 2, 1), grad_up


def solution(mesh):
    placed = (
        P(("dp", "fsdp"), None),
        P("fsdp", None),
        P("dp", "fsdp", None),
        P("dp", None, "fsdp"),
        P(("dp", "fsdp"), None),
        P(("dp", "fsdp")),
        P(("dp", "fsdp")),
    )
    return jax.shard_map(
        body,
        mesh=mesh,
        in_specs=placed,
        out_specs=(
            P(("dp", "fsdp"), None),
            P(("dp", "fsdp"), None),
            P("dp", "fsdp", None),
            P("dp", None, "fsdp"),
        ),
        check_vma=False,
    )
```
